32 devices in a mesh: parts: 2 (over x), freq: 16 (over z, y, core).
Axes of the slice: x: 2, y: 2, z: 4, core: 2. Of those that a mesh axis runs over, the one named last changes fastest.
Arguments:
- records: bfloat16 [2, 1024, 192, 128], P('parts', None, 'freq'), parts along dimension 0, may hold values from -6 to 6
- wavelet: float32 [2, 1024], P('parts'), parts along dimension 0, may hold values from -6 to 6
- offsets: int32 [2, 12, 8, 2], P('parts'), parts along dimension 0, may hold values from 0 to 15
- classes: int32 [8, 192, 128], P('parts'), parts along dimension 0, may hold values from 0 to 31
- coefficients: float32 [32, 64, 2, 9], P(None, 'freq'), may hold values from -2.5 to 2.5
Outputs:
- image: float32 [8, 192, 128], P('parts', 'freq'), parts along dimension 0
The draws below stay inside these ranges and needn't reach their ends.
There are 2 independent parts, one for each index of `parts`. The reference program is written for one: setup_inputs(seed, part) draws one part's arguments, and reference() takes and returns one part's arrays. A program takes and returns all parts, laid end to end along the dimension named above; an argument that names none is the same for every part. Nothing has to cross between parts.
Inputs may be any that keep to these rules, and one draw needn't show every extreme that they name: Each shot has exactly one source in every 16 x 16 block of the surface, at these offsets inside the block.
All inputs are finite; a program needn't handle non-finite values.
Results may differ from the reference program's by a relative error of at most 0.0023.
Values sent between devices are 32-bit elements; how exact they have to be, the bound alone decides.
A program may use at most 128 MiB of HBM per device.

```python
import math
import jax
import jax.numpy as jnp
from jax import lax

NX = 192
NY = 128
NT = 1024
NF = 64
SHOTS = 1
DEPTHS = 4
ORDER = 8
CLASSES = 32
SPACING = 16


def draw_records(key, part):
    jagged_key = jax.random.fold_in(key, 11)
    row_key = jax.random.fold_in(key, 12)
    column_key = jax.random.fold_in(key, 13)
    jagged = jax.random.normal(jagged_key, (SHOTS, NT, NX, NY), jnp.float32) * 0.5
    along_rows = jax.random.normal(row_key, (SHOTS, NT, NX, 1), jnp.float32) * 0.6
    along_columns = jax.random.normal(column_key, (SHOTS, NT, 1, NY), jnp.float32) * 0.6
    summed = jnp.clip(jagged + along_rows + along_columns, -6.0, 6.0)
    return summed.astype(jnp.bfloat16)


def draw_coefficients(key, part):
    degree = jnp.arange(ORDER + 1, dtype=jnp.int32)
    weights = jnp.where(degree == ORDER, 1.0, jnp.where(degree == ORDER - 1, 0.65, jnp.where(degree == ORDER - 2, 0.45, 0.1))).astype(jnp.float32)
    shared_key = jax.random.fold_in(key, 101)
    class_key = jax.random.fold_in(key, 202)
    shared = jax.random.normal(shared_key, (1, NF, 2, ORDER + 1), jnp.float32) * 0.6
    varied = jax.random.normal(class_key, (CLASSES, NF, 2, ORDER + 1), jnp.float32) * 0.35
    values = (shared + varied) * weights
    return jnp.clip(values, -2.5, 2.5).astype(jnp.float32)


def with_ends(drawn, stream_key, low, high):
    dims = drawn.shape
    place = [jax.random.randint(jax.random.fold_in(stream_key, axis), (), 0, dims[axis]) for axis in range(len(dims))]
    drawn = drawn.at[tuple(place)].set(low)
    longest = dims.index(max(dims))
    place[longest] = (place[longest] + 1) % dims[longest]
    return drawn.at[tuple(place)].set(high)


def bell_draw(key, shape, width, most, held_as=jnp.bfloat16):
    return jnp.clip(width * jax.random.normal(key, shape, jnp.float32), -most, most).astype(held_as)


def setup_inputs(seed: int = 0, part: int = 0) -> dict:
    splits = jax.random.split(jax.random.key(seed), 6)
    part_splits = jax.random.split(jax.random.fold_in(splits[5], part), 6)
    return {
        "records": draw_records(jax.random.fold_in(jax.random.fold_in(splits[5], part), 71), part),
        "wavelet": bell_draw(part_splits[1], (SHOTS, NT), 1.0, 6.0, jnp.float32),
        "offsets": with_ends(jax.random.randint(part_splits[2], (SHOTS, NX // SPACING, NY // SPACING, 2), 0, SPACING), jax.random.fold_in(part_splits[2], 1), 0, SPACING - 1).astype(jnp.int32),
        "classes": with_ends(jax.random.randint(part_splits[3], (DEPTHS, NX, NY), 0, CLASSES), jax.random.fold_in(part_splits[3], 1), 0, CLASSES - 1).astype(jnp.int32),
        "coefficients": draw_coefficients(jax.random.fold_in(splits[5], 71), part),
    }


first_bin = 4

def dft_table(count, record_duration):
    spectral_slots = jnp.arange(count, dtype=jnp.int32) + first_bin
    clock_moments = jnp.arange(record_duration, dtype=jnp.int32)
    elementwise_multiple = spectral_slots[:, None] * clock_moments[None, :] % record_duration
    phase = elementwise_multiple.astype(jnp.float32) * (2.0 * math.pi / record_duration)
    scaling = 1.0 / math.sqrt(record_duration)
    stacked = jnp.stack([jnp.cos(phase), -jnp.sin(phase)], axis=1) * scaling
    return stacked.reshape(2 * count, record_duration)

def mcclellan(field):
    widths = [(0, 0)] * (field.ndim - 2) + [(1, 1), (1, 1)]
    zero_extended = jnp.pad(field, widths)
    along_x = 0.25 * zero_extended[..., :-2, :] + 0.5 * zero_extended[..., 1:-1, :] + 0.25 * zero_extended[..., 2:, :]
    smoothed = 0.25 * along_x[..., :-2] + 0.5 * along_x[..., 1:-1] + 0.25 * along_x[..., 2:]
    return 2.0 * smoothed - field

def add_term(summed_terms, chebyshev, filters, degree):
    wavefield_polarity = jnp.array([1.0, -1.0], jnp.float32)[None, :, None, None, None]
    real_component = filters[:, 0, degree][:, None, None]
    im_part = filters[:, 1, degree][:, None, None] * wavefield_polarity
    cheb_re = chebyshev[:, :, :, 0]
    cheb_im = chebyshev[:, :, :, 1]
    return summed_terms + jnp.stack([real_component * cheb_re - im_part * cheb_im, real_component * cheb_im + im_part * cheb_re], axis=3)

def extrapolate(fields, filters):
    degrees = filters.shape[2]
    previous = fields
    current = mcclellan(fields)
    summed_terms = add_term(jnp.zeros_like(fields), previous, filters, 0)
    summed_terms = add_term(summed_terms, current, filters, 1)
    for degree in range(2, degrees):
        previous, current = (current, 2.0 * mcclellan(current) - previous)
        summed_terms = add_term(summed_terms, current, filters, degree)
    return summed_terms

def emitter_impulses(offsets, spacing, height, breadth):
    off_x = jnp.repeat(jnp.repeat(offsets[..., 0], spacing, axis=1), spacing, axis=2)
    off_y = jnp.repeat(jnp.repeat(offsets[..., 1], spacing, axis=1), spacing, axis=2)
    row_phase = jnp.arange(height, dtype=jnp.int32) % spacing
    col_phase = jnp.arange(breadth, dtype=jnp.int32) % spacing
    hits = (row_phase[None, :, None] == off_x) & (col_phase[None, None, :] == off_y)
    return hits.astype(jnp.float32)

def reference(records, wavelet, offsets, classes, coefficients):
    fourier_matrix = dft_table(NF, NT)
    narrow_table = fourier_matrix.astype(jnp.bfloat16)
    spectra = jnp.stack([jnp.dot(narrow_table, records[shot].reshape(NT, NX * NY), preferred_element_type=jnp.float32).reshape(NF, 2, NX, NY) for shot in range(SHOTS)], axis=1)
    wave_spec = jnp.dot(wavelet, fourier_matrix.T, precision=lax.Precision.HIGHEST).reshape(SHOTS, NF, 2).transpose(1, 0, 2)
    spikes = emitter_impulses(offsets, SPACING, NX, NY)
    class_ids = jnp.arange(CLASSES, dtype=jnp.int32)

    def one_frequency(inputs):
        received, single_wavefield, table_one = inputs
        source = single_wavefield[:, :, None, None] * spikes[:, None]
        fields = jnp.stack([source, received], axis=0)[None]
        migrated_pictures = []
        for level in range(DEPTHS):
            onehot = (classes[level][None] == class_ids[:, None, None]).astype(jnp.float32)
            filters = jnp.einsum('crk,cxy->rkxy', table_one, onehot, precision=lax.Precision.HIGHEST)[None]
            fields = extrapolate(fields, filters)
            migrated_pictures.append(lax.optimization_barrier(jnp.sum(fields[:, 0] * fields[:, 1], axis=(0, 1, 2))))
        return jnp.stack(migrated_pictures)
    per_freq = lax.map(one_frequency, (spectra, wave_spec, jnp.transpose(coefficients, (1, 0, 2, 3))))
    return lax.optimization_barrier(jnp.sum(per_freq, axis=0))
```

```python
import functools
import math

import jax
import jax.numpy as jnp
import numpy as np
from jax import lax
from jax.experimental import pallas as pl
from jax.experimental.pallas import tpu as pltpu
from jax.sharding import PartitionSpec as P

NF = 64
SPACING = 16
LANES = 128
SUBS = 8
NODES = (0.0, 1.0)


first_bin = 4


def dft_rows(count, record_duration):
    slots = np.arange(count, dtype=np.int64) + first_bin
    moments = np.arange(record_duration, dtype=np.int64)
    phase = (slots[:, None] * moments[None, :] % record_duration).astype(np.float32)
    phase = phase * np.float32(2.0 * math.pi / record_duration)
    scaling = np.float32(1.0 / math.sqrt(record_duration))
    return np.cos(phase) * scaling, -np.sin(phase) * scaling


def basis_change(degrees):
    poly = np.polynomial.Polynomial
    basis = [poly([1.0])]
    for j in range(degrees - 1):
        basis.append(basis[-1] * poly([-16.0 * NODES[j % 2], 16.0]))
    matrix = np.zeros((degrees, degrees))
    for j, b in enumerate(basis):
        matrix[: len(b.coef), j] = b.coef
    out = np.zeros((degrees, degrees))
    for k in range(degrees):
        shifted = np.polynomial.Chebyshev.basis(k).convert(kind=poly)(poly([-1.0, 2.0]))
        coef = np.zeros(degrees)
        coef[: len(shifted.coef)] = shifted.coef
        out[:, k] = np.linalg.solve(matrix, coef)
    return out


def iotas():
    lane = lax.broadcasted_iota(jnp.int32, (SUBS, LANES), 1)
    sub = lax.broadcasted_iota(jnp.int32, (SUBS, LANES), 0)
    return lane, sub


def pick(table, index):
    along_lanes = lax.GatherDimensionNumbers(
        offset_dims=(),
        collapsed_slice_dims=(1,),
        start_index_map=(1,),
        operand_batching_dims=(0,),
        start_indices_batching_dims=(0,),
    )
    return lax.gather(
        table,
        index[..., None],
        along_lanes,
        slice_sizes=(1, 1),
        mode=lax.GatherScatterMode.PROMISE_IN_BOUNDS,
    )


def row_of(tab, part, k):
    return jnp.broadcast_to(tab[part, pl.ds(k, 1), :], (SUBS, LANES))


def lane_classes(classes, idx, flat, group, class_count):
    depths, nx, ny = idx.shape[:3]
    blocks = LANES // group
    lane, _ = iotas()
    places = [(d, x) for d in range(depths) for x in range(nx)]
    for n in range(0, len(places), group):
        some = places[n : n + group]
        rows = [classes[d, pl.ds(x, blocks, stride=nx), :] for d, x in some]
        slot = n // group % 2
        flat[slot] = jnp.transpose(jnp.concatenate(rows, axis=0).astype(jnp.float32))
        for y in range(ny):
            line = flat[slot, pl.ds(y, SUBS, stride=ny), :].astype(jnp.int32)
            for i, (d, x) in enumerate(some):
                idx[d, x, y] = pick(line, lane // group + i * blocks) + lane % group * class_count


def degree_pass(cur, planes, acc, tab, k, idx, node, group, nx, ny):
    lane, sub = iotas()
    low, high = lane >= group, lane < LANES - group
    first, last = sub >= 1, sub < SUBS - 1
    gr, gi = row_of(tab, 0, k), row_of(tab, 1, k)

    def along_x(c, y):
        v = [cur[c, x, y] for x in range(nx)]
        before = jnp.where(low, pltpu.roll(v[nx - 1], group, 1), 0.0)
        after = jnp.where(high, pltpu.roll(v[0], LANES - group, 1), 0.0)
        ext = [before] + v + [after]
        pair = [ext[i] + ext[i + 1] for i in range(nx + 1)]
        return [pair[i] + pair[i + 1] for i in range(nx)]

    u, q, u_first = [], [], []
    for c in range(planes):
        end = along_x(c, ny - 1)
        prev = [jnp.where(first, pltpu.roll(e, 1, 0), 0.0) for e in end]
        start = along_x(c, 0)
        u.append(start)
        u_first.append(start)
        q.append([a + b for a, b in zip(prev, start)])
    for y in range(ny):
        made = []
        for c in range(planes):
            if y < ny - 1:
                nxt = along_x(c, y + 1)
            else:
                nxt = [jnp.where(last, pltpu.roll(e, SUBS - 1, 0), 0.0) for e in u_first[c]]
            q_next = [a + b for a, b in zip(u[c], nxt)]
            total = [a + b for a, b in zip(q[c], q_next)]
            if node:
                total = [t - (16.0 * node) * cur[c, x, y] for x, t in enumerate(total)]
            for x in range(nx):
                cur[c, x, y] = total[x]
            made.append(total)
            u[c], q[c] = nxt, q_next
        for x in range(nx):
            hr, hi = pick(gr, idx[x, y]), pick(gi, idx[x, y])
            if planes == 2:
                re, im = made[0][x], made[1][x]
                acc[0, x, y] = acc[0, x, y] + (hr * re - hi * im)
                acc[1, x, y] = acc[1, x, y] + (hr * im + hi * re)
            else:
                acc[0, x, y] = acc[0, x, y] + hr * made[0][x]
                acc[1, x, y] = acc[1, x, y] + hi * made[0][x]


def all_degrees(cur, planes, acc, tab, idx, group, nx, ny, degrees):
    def two(j, carry):
        degree_pass(cur, planes, acc, tab, 2 * j + 1, idx, NODES[0], group, nx, ny)
        degree_pass(cur, planes, acc, tab, 2 * j + 2, idx, NODES[1], group, nx, ny)
        return carry

    lax.fori_loop(0, (degrees - 1) // 2, two, 0)
    if degrees % 2 == 0:
        degree_pass(cur, planes, acc, tab, degrees - 1, idx, NODES[0], group, nx, ny)


def degree_zero(cur, acc, tab, idx, nx, ny, load):
    gr, gi = row_of(tab, 0, 0), row_of(tab, 1, 0)

    def row(y, carry):
        for x in range(nx):
            re, im = load(x, y)
            cur[0, x, y] = re
            cur[1, x, y] = im
            hr, hi = pick(gr, idx[x, y]), pick(gi, idx[x, y])
            acc[0, x, y] = hr * re - hi * im
            acc[1, x, y] = hr * im + hi * re
        return carry

    lax.fori_loop(0, ny, row, 0, unroll=2)


def source_kernel(group, class_count, off_ref, wave_ref, tab, classes, out, idx, cur, flat):
    depths, nx, ny = idx.shape[:3]
    degrees = tab.shape[1]
    lane, _ = iotas()
    lane_classes(classes, idx, flat, group, class_count)
    gr, gi = row_of(tab, 0, 0), row_of(tab, 1, 0)
    row_x = [lane // group * nx + x for x in range(nx)]
    off_x = [pick(off_ref[0], r // SPACING) for r in row_x]
    off_y = [pick(off_ref[1], r // SPACING) for r in row_x]

    def spike_row(y, carry):
        for x in range(nx):
            hit = (row_x[x] % SPACING == off_x[x]) & (off_y[x] == y)
            v = jnp.where(hit, 1.0, 0.0)
            cur[0, x, y] = v
            out[0, 0, x, y] = pick(gr, idx[0, x, y]) * v
            out[0, 1, x, y] = pick(gi, idx[0, x, y]) * v
        return carry

    lax.fori_loop(0, ny, spike_row, 0, unroll=2)
    all_degrees(cur, 1, out.at[0], tab, idx.at[0], group, nx, ny, degrees)
    wr, wi = jnp.zeros((SUBS, LANES), jnp.float32), jnp.zeros((SUBS, LANES), jnp.float32)
    for f in range(group):
        wr = jnp.where(lane % group == f, wave_ref[f], wr)
        wi = jnp.where(lane % group == f, -wave_ref[group + f], wi)

    def wave_row(y, carry):
        for x in range(nx):
            re, im = out[0, 0, x, y], out[0, 1, x, y]
            out[0, 0, x, y] = wr * re - wi * im
            out[0, 1, x, y] = wr * im + wi * re
        return carry

    lax.fori_loop(0, ny, wave_row, 0, unroll=2)

    def depth(d, carry):
        def load(x, y):
            return out[d - 1, 0, x, y], out[d - 1, 1, x, y]

        degree_zero(cur, out.at[d], tab, idx.at[d], nx, ny, load)
        all_degrees(cur, 2, out.at[d], tab, idx.at[d], group, nx, ny, degrees)
        return carry

    lax.fori_loop(1, depths, depth, 0)


def exchange_peers(ranks):
    me = lax.axis_index("freq")
    return me, [lax.rem(me + k, ranks) for k in range(1, ranks)]


def remote(src, dst, send, recv, peer):
    return pltpu.make_async_remote_copy(
        src_ref=src,
        dst_ref=dst,
        send_sem=send,
        recv_sem=recv,
        device_id={"freq": peer},
        device_id_type=pl.DeviceIdType.MESH,
    )


def unpack_received(received, acc, flat, group, nx, ny):
    senders = received.shape[0]
    sub3 = lax.broadcasted_iota(jnp.int32, (senders, SUBS, LANES), 1)
    upper = sub3 < group
    for x in range(nx):
        a, b = received[:, x], received[:, nx + x]
        parts = (
            jnp.where(upper, a, pltpu.roll(b, group, 1)),
            jnp.where(upper, pltpu.roll(a, group, 1), b),
        )
        for r in range(2):
            flat[r] = jnp.transpose(parts[r].reshape(LANES, LANES))
            for y in range(ny):
                acc[r, x, y] = flat[r, pl.ds(y, SUBS, stride=ny), :]


def form_image(src, acc, flat, turned, image, group, nx, ny):
    owners = image.shape[0] // 16
    for x in range(nx):
        for y in range(ny):
            v = src[0, x, y] * acc[0, x, y] - src[1, x, y] * acc[1, x, y]
            shift = 1
            while shift < group:
                v = v + pltpu.roll(v, shift, 1)
                shift *= 2
            flat[x % 2, pl.ds(y, SUBS, stride=ny), :] = v
        turned[x % 2] = jnp.transpose(flat[x % 2])
        for b in range(2):
            lane = b * group + group - 1
            image[pl.ds(b * nx + x, owners, stride=16), :] = (
                turned[x % 2, pl.ds(lane, owners, stride=2 * group), :]
            )


def migrate_kernel(
    group, class_count, ranks,
    off_ref, wave_ref, tab, classes, spectra,
    out,
    src, idx, cur, acc, flat, turned, received, image, slots,
    local_sem, a_send, a_recv, i_send, i_recv,
):
    depths, nx, ny = idx.shape[:3]
    degrees = tab.shape[1]
    me, peers = exchange_peers(ranks)
    barrier = pltpu.get_barrier_semaphore()
    for peer in peers:
        pl.semaphore_signal(
            barrier, inc=1, device_id={"freq": peer}, device_id_type=pl.DeviceIdType.MESH
        )
    pl.semaphore_wait(barrier, ranks - 1)
    own = pltpu.make_async_copy(spectra.at[me], received.at[me], local_sem)
    own.start()
    fields = []
    for k, peer in enumerate(peers):
        copy = remote(spectra.at[peer], received.at[me], a_send.at[k], a_recv.at[k], peer)
        copy.start()
        fields.append(copy)
    source_kernel(group, class_count, off_ref, wave_ref, tab, classes, src, idx, cur, flat)
    own.wait()
    for copy in fields:
        copy.wait()
    unpack_received(received, acc, flat, group, nx, ny)

    def sends(d):
        return [
            remote(
                image.at[d, pl.ds(peer * 16, 16)],
                slots.at[d, k],
                i_send.at[d, k],
                i_recv.at[d, k],
                peer,
            )
            for k, peer in enumerate(peers)
        ]

    def depth(d, carry):
        degree_zero(cur, acc, tab, idx.at[d], nx, ny, lambda x, y: (acc[0, x, y], acc[1, x, y]))
        all_degrees(cur, 2, acc, tab, idx.at[d], group, nx, ny, degrees)
        form_image(src.at[d], acc, flat, turned, image.at[d], group, nx, ny)
        for copy in sends(d):
            copy.start()
        return carry

    lax.fori_loop(0, depths, depth, 0)
    tile = out.shape[1]
    for d in range(depths):
        total = image[d, pl.ds(me * 16, 16), :]
        for k, copy in enumerate(sends(d)):
            copy.wait_recv()
            total = total + slots[d, k]
        out[d] = total[:tile]
    for d in range(depths):
        for copy in sends(d):
            copy.wait_send()


def fast_device(records, wavelet, offsets, classes, coefficients):
    _, record_duration, tile_rows, width = records.shape
    depths, height, _ = classes.shape
    class_count, group, _, degrees = coefficients.shape
    ranks = height // tile_rows
    nx, ny = group * height // LANES, width // SUBS
    cos_rows, sin_rows = dft_rows(NF, record_duration)
    pair = np.stack(
        [cos_rows.reshape(ranks, group, -1), -sin_rows.reshape(ranks, group, -1)], axis=1
    ).reshape(ranks, 2 * group, record_duration)
    narrow = jnp.asarray(pair).astype(jnp.bfloat16)
    spectra = jnp.einsum(
        "jqt,txy->jxqy", narrow, records[0], preferred_element_type=jnp.float32
    )

    mine = lax.dynamic_index_in_dim(jnp.asarray(pair), lax.axis_index("freq"), 0, keepdims=False)
    wave = jnp.sum(mine * wavelet, axis=1)
    off = offsets[0].transpose(2, 1, 0)
    off = jnp.pad(off, ((0, 0), (0, 0), (0, LANES - off.shape[2])))
    change = jnp.asarray(basis_change(degrees), jnp.float32)
    tab = jnp.einsum("jk,cfrk->rjfc", change, coefficients, precision=lax.Precision.HIGHEST)
    tab = tab.reshape(2, degrees, group * class_count)
    tab = jnp.pad(tab, ((0, 0), (0, 0), (0, LANES - group * class_count)))

    plane = (2, nx, ny, SUBS, LANES)
    square = pltpu.VMEM((2, LANES, LANES), jnp.float32)
    vmem = pl.BlockSpec(memory_space=pltpu.VMEM)
    smem = pl.BlockSpec(memory_space=pltpu.SMEM)
    return pl.pallas_call(
        functools.partial(migrate_kernel, group, class_count, ranks),
        out_shape=jax.ShapeDtypeStruct((depths, tile_rows, width), jnp.float32),
        in_specs=[vmem, smem, vmem, vmem, vmem],
        out_specs=vmem,
        scratch_shapes=[
            pltpu.VMEM((depths,) + plane, jnp.float32),
            pltpu.VMEM((depths,) + plane[1:], jnp.int32),
            pltpu.VMEM(plane, jnp.float32),
            pltpu.VMEM(plane, jnp.float32),
            square,
            square,
            pltpu.VMEM(spectra.shape, jnp.float32),
            pltpu.VMEM((depths, ranks * 16, width), jnp.float32),
            pltpu.VMEM((depths, ranks - 1, 16, width), jnp.float32),
            pltpu.SemaphoreType.DMA,
            pltpu.SemaphoreType.DMA((ranks - 1,)),
            pltpu.SemaphoreType.DMA((ranks - 1,)),
            pltpu.SemaphoreType.DMA((depths, ranks - 1)),
            pltpu.SemaphoreType.DMA((depths, ranks - 1)),
        ],
        compiler_params=pltpu.CompilerParams(collective_id=0, has_side_effects=True),
        name="migrate",
    )(off, wave, tab, classes, spectra)


def dft_table(count, record_duration):
    spectral_slots = jnp.arange(count, dtype=jnp.int32) + first_bin
    clock_moments = jnp.arange(record_duration, dtype=jnp.int32)
    elementwise_multiple = spectral_slots[:, None] * clock_moments[None, :] % record_duration
    phase = elementwise_multiple.astype(jnp.float32) * (2.0 * math.pi / record_duration)
    scaling = 1.0 / math.sqrt(record_duration)
    stacked = jnp.stack([jnp.cos(phase), -jnp.sin(phase)], axis=1) * scaling
    return stacked.reshape(2 * count, record_duration)


def mcclellan(field):
    widths = [(0, 0)] * (field.ndim - 2) + [(1, 1), (1, 1)]
    zero_extended = jnp.pad(field, widths)
    along_x = (
        0.25 * zero_extended[..., :-2, :]
        + 0.5 * zero_extended[..., 1:-1, :]
        + 0.25 * zero_extended[..., 2:, :]
    )
    smoothed = 0.25 * along_x[..., :-2] + 0.5 * along_x[..., 1:-1] + 0.25 * along_x[..., 2:]
    return 2.0 * smoothed - field


def add_term(summed_terms, chebyshev, filters, degree):
    wavefield_polarity = jnp.array([1.0, -1.0], jnp.float32)[None, :, None, None, None]
    real_component = filters[:, 0, degree][:, None, None]
    im_part = filters[:, 1, degree][:, None, None] * wavefield_polarity
    cheb_re = chebyshev[:, :, :, 0]
    cheb_im = chebyshev[:, :, :, 1]
    return summed_terms + jnp.stack(
        [
            real_component * cheb_re - im_part * cheb_im,
            real_component * cheb_im + im_part * cheb_re,
        ],
        axis=3,
    )


def extrapolate(fields, filters):
    degrees = filters.shape[2]
    previous = fields
    current = mcclellan(fields)
    summed_terms = add_term(jnp.zeros_like(fields), previous, filters, 0)
    summed_terms = add_term(summed_terms, current, filters, 1)
    for degree in range(2, degrees):
        previous, current = (current, 2.0 * mcclellan(current) - previous)
        summed_terms = add_term(summed_terms, current, filters, degree)
    return summed_terms


def emitter_impulses(offsets, spacing, height, breadth):
    off_x = jnp.repeat(jnp.repeat(offsets[..., 0], spacing, axis=1), spacing, axis=2)
    off_y = jnp.repeat(jnp.repeat(offsets[..., 1], spacing, axis=1), spacing, axis=2)
    row_phase = jnp.arange(height, dtype=jnp.int32) % spacing
    col_phase = jnp.arange(breadth, dtype=jnp.int32) % spacing
    hits = (row_phase[None, :, None] == off_x) & (col_phase[None, None, :] == off_y)
    return hits.astype(jnp.float32)


def plain_device(records, wavelet, offsets, classes, coefficients):
    shot_count, record_duration, tile_rows, width_y = records.shape
    freq_local = coefficients.shape[1]
    fourier_matrix = dft_table(NF, record_duration)
    narrow_table = fourier_matrix.astype(jnp.bfloat16)
    spectra = jnp.stack(
        [
            jnp.dot(
                narrow_table,
                records[0].reshape(record_duration, tile_rows * width_y),
                preferred_element_type=jnp.float32,
            ).reshape(NF, 2, tile_rows, width_y)
        ],
        axis=1,
    )
    receivers = lax.all_to_all(spectra, "freq", split_axis=0, concat_axis=3, tiled=True)
    height = receivers.shape[3]
    wave_spec = (
        jnp.dot(wavelet, fourier_matrix.T, precision=lax.Precision.HIGHEST)
        .reshape(shot_count, NF, 2)
        .transpose(1, 0, 2)
    )
    first_freq = lax.axis_index("freq") * freq_local
    wave_local = lax.dynamic_slice_in_dim(wave_spec, first_freq, freq_local, 0)
    spikes = emitter_impulses(offsets, SPACING, height, width_y)
    source = wave_local[:, :, :, None, None] * spikes[None, :, None]
    fields = jnp.stack([source, receivers], axis=1)
    class_ids = jnp.arange(coefficients.shape[0], dtype=jnp.int32)
    migrated_pictures = []
    for level in range(classes.shape[0]):
        onehot = (classes[level][None] == class_ids[:, None, None]).astype(jnp.float32)
        filters = jnp.einsum(
            "cfrk,cxy->frkxy", coefficients, onehot, precision=lax.Precision.HIGHEST
        )
        fields = extrapolate(fields, filters)
        partial_value = jnp.sum(fields[:, 0] * fields[:, 1], axis=(0, 1, 2))
        migrated_pictures.append(
            lax.psum_scatter(partial_value, "freq", scatter_dimension=0, tiled=True)
        )
    return jnp.stack(migrated_pictures)


def fits_lanes(records, classes, coefficients):
    tile_rows, width = records.shape[2:]
    height = classes.shape[1]
    class_count, group = coefficients.shape[:2]
    return (
        2 * group == SUBS
        and width == LANES
        and width // SUBS == SPACING
        and group * class_count <= LANES
        and height * group % LANES == 0
        and height // tile_rows % 2 == 0
        and 2 * (height * group // LANES) == tile_rows
    )


def per_device(records, wavelet, offsets, classes, coefficients):
    if fits_lanes(records, classes, coefficients):
        return fast_device(records, wavelet, offsets, classes, coefficients)
    return plain_device(records, wavelet, offsets, classes, coefficients)


def solution(mesh):
    placed = (
        P("parts", None, "freq", None),
        P("parts", None),
        P("parts", None, None, None),
        P("parts", None, None),
        P(None, "freq", None, None),
    )
    return jax.shard_map(
        per_device, mesh=mesh, in_specs=placed, out_specs=P("parts", "freq", None), check_vma=False
    )
```

```python
import functools
import math

import jax
import jax.numpy as jnp
import numpy as np
from jax import lax
from jax.experimental import pallas as pl
from jax.experimental.pallas import tpu as pltpu
from jax.sharding import PartitionSpec as P

NF = 64
SPACING = 16
LANES = 128
SUBS = 8
VMEM_BYTES = 60 * 2**20
NODES = (0.75, 1.0)


first_bin = 4


def dft_rows(count, record_duration):
    slots = np.arange(count, dtype=np.int64) + first_bin
    moments = np.arange(record_duration, dtype=np.int64)
    phase = (slots[:, None] * moments[None, :] % record_duration).astype(np.float32)
    phase = phase * np.float32(2.0 * math.pi / record_duration)
    scaling = np.float32(1.0 / math.sqrt(record_duration))
    return np.cos(phase) * scaling, -np.sin(phase) * scaling


def basis_change(degrees):
    poly = np.polynomial.Polynomial
    basis = [poly([1.0])]
    for j in range(degrees - 1):
        node = NODES[j] if j < len(NODES) else 0.0
        basis.append(basis[-1] * poly([-16.0 * node, 16.0]))
    matrix = np.zeros((degrees, degrees))
    for j, b in enumerate(basis):
        matrix[: len(b.coef), j] = b.coef
    out = np.zeros((degrees, degrees))
    for k in range(degrees):
        shifted = np.polynomial.Chebyshev.basis(k).convert(kind=poly)(poly([-1.0, 2.0]))
        coef = np.zeros(degrees)
        coef[: len(shifted.coef)] = shifted.coef
        out[:, k] = np.linalg.solve(matrix, coef)
    return out


def iotas():
    lane = lax.broadcasted_iota(jnp.int32, (SUBS, LANES), 1)
    sub = lax.broadcasted_iota(jnp.int32, (SUBS, LANES), 0)
    return lane, sub


def pick(table, index):
    along_lanes = lax.GatherDimensionNumbers(
        offset_dims=(),
        collapsed_slice_dims=(1,),
        start_index_map=(1,),
        operand_batching_dims=(0,),
        start_indices_batching_dims=(0,),
    )
    return lax.gather(
        table,
        index[..., None],
        along_lanes,
        slice_sizes=(1, 1),
        mode=lax.GatherScatterMode.PROMISE_IN_BOUNDS,
    )


def row_of(tab, part, k):
    return jnp.broadcast_to(tab[part, pl.ds(k, 1), :], (SUBS, LANES))


def lane_classes(classes, idx, flat, group, class_count):
    depths, nx, ny = idx.shape[:3]
    blocks = LANES // group
    lane, _ = iotas()
    places = [(d, x) for d in range(depths) for x in range(nx)]
    for n in range(0, len(places), group):
        some = places[n : n + group]
        rows = [classes[d, pl.ds(x, blocks, stride=nx), :] for d, x in some]
        slot = n // group % 2
        flat[slot] = jnp.transpose(jnp.concatenate(rows, axis=0).astype(jnp.float32))
        for i, (d, x) in enumerate(some):
            for y in range(ny):
                line = flat[slot, pl.ds(y, SUBS, stride=ny), :].astype(jnp.int32)
                idx[d, x, y] = pick(line, lane // group + i * blocks) + lane % group * class_count


def look_up(tab, idx, filters, x, y):
    degrees = tab.shape[1]
    place = idx[x, y]
    for k in range(degrees):
        for part in range(2):
            filters[k, part, x, y] = pick(row_of(tab, part, k), place)


def degree_pass(cur, planes, acc, filters, node, group, nx, ny, beside):
    lane, sub = iotas()
    low, high = lane >= group, lane < LANES - group
    first, last = sub >= 1, sub < SUBS - 1

    def along_x(c, y):
        v = [cur[c, x, y] for x in range(nx)]
        before = jnp.where(low, pltpu.roll(v[nx - 1], group, 1), 0.0)
        after = jnp.where(high, pltpu.roll(v[0], LANES - group, 1), 0.0)
        ext = [before] + v + [after]
        pair = [ext[i] + ext[i + 1] for i in range(nx + 1)]
        return [pair[i] + pair[i + 1] for i in range(nx)]

    u, q, u_first = [], [], []
    for c in range(planes):
        end = along_x(c, ny - 1)
        prev = [jnp.where(first, pltpu.roll(e, 1, 0), 0.0) for e in end]
        start = along_x(c, 0)
        u.append(start)
        u_first.append(start)
        q.append([a + b for a, b in zip(prev, start)])
    for y in range(ny):
        made = []
        for c in range(planes):
            if y < ny - 1:
                nxt = along_x(c, y + 1)
            else:
                nxt = [jnp.where(last, pltpu.roll(e, SUBS - 1, 0), 0.0) for e in u_first[c]]
            q_next = [a + b for a, b in zip(u[c], nxt)]
            total = [a + b for a, b in zip(q[c], q_next)]
            if node is not None:
                total = [t - node * cur[c, x, y] for x, t in enumerate(total)]
            for x in range(nx):
                cur[c, x, y] = total[x]
            made.append(total)
            u[c], q[c] = nxt, q_next
        for x in range(nx):
            hr, hi = filters[0, x, y], filters[1, x, y]
            if planes == 2:
                re, im = made[0][x], made[1][x]
                acc[0, x, y] = acc[0, x, y] + (hr * re - hi * im)
                acc[1, x, y] = acc[1, x, y] + (hr * im + hi * re)
            else:
                acc[0, x, y] = acc[0, x, y] + hr * made[0][x]
                acc[1, x, y] = acc[1, x, y] + hi * made[0][x]
        beside(y)


def all_degrees(cur, planes, acc, filters, group, nx, ny, ahead=None):
    steps = filters.shape[0] - 1
    share = nx * ny // steps

    def one(shifted, j, carry):
        def beside(y):
            if ahead is not None:
                for n in range(share * y // ny, share * (y + 1) // ny):
                    ahead(n % nx, j * (share // nx) + n // nx)

        node = None
        if shifted:
            node = jnp.float32(16.0 * NODES[-1])
            for n, value in enumerate(NODES[:-1]):
                node = jnp.where(j == n, jnp.float32(16.0 * value), node)
        degree_pass(cur, planes, acc, filters.at[j + 1], node, group, nx, ny, beside)
        return carry

    lax.fori_loop(0, len(NODES), functools.partial(one, True), 0)
    lax.fori_loop(len(NODES), steps, functools.partial(one, False), 0)


def degree_zero(cur, acc, filters, nx, ny, load):
    def row(y, carry):
        for x in range(nx):
            re, im = load(x, y)
            cur[0, x, y] = re
            cur[1, x, y] = im
            hr, hi = filters[0, 0, x, y], filters[0, 1, x, y]
            acc[0, x, y] = hr * re - hi * im
            acc[1, x, y] = hr * im + hi * re
        return carry

    lax.fori_loop(0, ny, row, 0, unroll=2)


def source_steps(group, off_ref, wave_ref, tab, out, idx, filters, cur):
    depths, nx, ny = idx.shape[:3]
    lane, _ = iotas()

    def first(y, carry):
        for x in range(nx):
            look_up(tab, idx.at[0], filters.at[0], x, y)
        return carry

    lax.fori_loop(0, ny, first, 0)
    row_x = [lane // group * nx + x for x in range(nx)]
    off_x = [pick(off_ref[0], r // SPACING) for r in row_x]
    off_y = [pick(off_ref[1], r // SPACING) for r in row_x]

    def spike_row(y, carry):
        for x in range(nx):
            hit = (row_x[x] % SPACING == off_x[x]) & (off_y[x] == y)
            v = jnp.where(hit, 1.0, 0.0)
            cur[0, x, y] = v
            out[0, 0, x, y] = filters[0, 0, 0, x, y] * v
            out[0, 1, x, y] = filters[0, 0, 1, x, y] * v
        return carry

    lax.fori_loop(0, ny, spike_row, 0, unroll=2)

    def ahead_of(d):
        return functools.partial(look_up, tab, idx.at[d], filters.at[d])

    all_degrees(cur, 1, out.at[0], filters.at[0], group, nx, ny, ahead_of(1))
    wr, wi = jnp.zeros((SUBS, LANES), jnp.float32), jnp.zeros((SUBS, LANES), jnp.float32)
    for f in range(group):
        wr = jnp.where(lane % group == f, wave_ref[f], wr)
        wi = jnp.where(lane % group == f, -wave_ref[group + f], wi)

    def wave_row(y, carry):
        for x in range(nx):
            re, im = out[0, 0, x, y], out[0, 1, x, y]
            out[0, 0, x, y] = wr * re - wi * im
            out[0, 1, x, y] = wr * im + wi * re
        return carry

    lax.fori_loop(0, ny, wave_row, 0, unroll=2)

    def depth(d, carry):
        filter_step(group, cur, out.at[d - 1], out.at[d], filters.at[d], ahead_of(d + 1))
        return carry

    lax.fori_loop(1, depths - 1, depth, 0)


def filter_step(group, cur, begin, end, filters, ahead=None):
    nx, ny = begin.shape[1:3]
    degree_zero(cur, end, filters, nx, ny, lambda x, y: (begin[0, x, y], begin[1, x, y]))
    all_degrees(cur, 2, end, filters, group, nx, ny, ahead)


def exchange_peers(ranks):
    me = lax.axis_index("freq")
    return me, [lax.rem(me + k, ranks) for k in range(1, ranks)]


def remote(src, dst, send, recv, peer):
    return pltpu.make_async_remote_copy(
        src_ref=src,
        dst_ref=dst,
        send_sem=send,
        recv_sem=recv,
        device_id={"freq": peer},
        device_id_type=pl.DeviceIdType.MESH,
    )


def unpack_received(received, acc, flat, group, nx, ny):
    senders = received.shape[0]
    sub3 = lax.broadcasted_iota(jnp.int32, (senders, SUBS, LANES), 1)
    upper = sub3 < group
    for x in range(nx):
        a, b = received[:, x], received[:, nx + x]
        parts = (
            jnp.where(upper, a, pltpu.roll(b, group, 1)),
            jnp.where(upper, pltpu.roll(a, group, 1), b),
        )
        for r in range(2):
            flat[r] = jnp.transpose(parts[r].reshape(LANES, LANES))
            for y in range(ny):
                acc[r, x, y] = flat[r, pl.ds(y, SUBS, stride=ny), :]


def form_image(src, acc, flat, turned, image, group, nx, ny):
    owners = image.shape[0] // 16
    for x in range(nx):
        for y in range(ny):
            v = src[0, x, y] * acc[0, x, y] - src[1, x, y] * acc[1, x, y]
            shift = 1
            while shift < group:
                v = v + pltpu.roll(v, shift, 1)
                shift *= 2
            flat[x % 2, pl.ds(y, SUBS, stride=ny), :] = v
        turned[x % 2] = jnp.transpose(flat[x % 2])
        for b in range(2):
            lane = b * group + group - 1
            image[pl.ds(b * nx + x, owners, stride=16), :] = (
                turned[x % 2, pl.ds(lane, owners, stride=2 * group), :]
            )


def migrate_kernel(
    group, class_count, ranks,
    off_ref, wave_ref, tab, classes, spectra,
    out,
    fields, idx, filters, cur, flat, turned, received, image, slots,
    local_sem, a_send, a_recv, i_send, i_recv,
):
    depths, nx, ny = idx.shape[:3]
    me, peers = exchange_peers(ranks)
    barrier = pltpu.get_barrier_semaphore()
    for peer in peers:
        pl.semaphore_signal(
            barrier, inc=1, device_id={"freq": peer}, device_id_type=pl.DeviceIdType.MESH
        )
    pl.semaphore_wait(barrier, ranks - 1)
    own = pltpu.make_async_copy(spectra.at[me], received.at[me], local_sem)
    own.start()
    spread = [
        remote(spectra.at[peer], received.at[me], a_send.at[k], a_recv.at[k], peer)
        for k, peer in enumerate(peers)
    ]
    for copy in spread:
        copy.start()
    lane_classes(classes, idx, flat, group, class_count)
    source_steps(group, off_ref, wave_ref, tab, fields, idx, filters, cur)
    acc = fields.at[depths]
    def sends(d):
        return [
            remote(
                image.at[d, pl.ds(peer * 16, 16)],
                slots.at[d, k],
                i_send.at[d, k],
                i_recv.at[d, k],
                peer,
            )
            for k, peer in enumerate(peers)
        ]

    def step(n, carry):
        @pl.when(n == 1)
        def _():
            own.wait()
            for copy in spread:
                copy.wait()
            unpack_received(received, acc, flat, group, nx, ny)

        ready = jnp.minimum(n, 1)
        begin = (depths - 2) * (1 - ready) + depths * ready
        end = depths - 1 + ready
        d = (depths - 1) * (1 - ready) + (n - 1) * ready
        filter_step(group, cur, fields.at[begin], fields.at[end], filters.at[d])

        @pl.when(n >= 1)
        def _():
            form_image(fields.at[d], acc, flat, turned, image.at[d], group, nx, ny)
            for copy in sends(d):
                copy.start()

        return carry

    lax.fori_loop(0, depths + 1, step, 0)
    tile = out.shape[1]
    for d in range(depths):
        total = image[d, pl.ds(me * 16, 16), :]
        for k, copy in enumerate(sends(d)):
            copy.wait_recv()
            total = total + slots[d, k]
        out[d] = total[:tile]
    for d in range(depths):
        for copy in sends(d):
            copy.wait_send()


def fast_device(records, wavelet, offsets, classes, coefficients):
    _, record_duration, tile_rows, width = records.shape
    depths, height, _ = classes.shape
    class_count, group, _, degrees = coefficients.shape
    ranks = height // tile_rows
    nx, ny = group * height // LANES, width // SUBS
    cos_rows, sin_rows = dft_rows(NF, record_duration)
    pair = np.stack(
        [cos_rows.reshape(ranks, group, -1), -sin_rows.reshape(ranks, group, -1)], axis=1
    ).reshape(ranks, 2 * group, record_duration)
    narrow = jnp.asarray(pair).astype(jnp.bfloat16)
    spectra = jnp.einsum(
        "jqt,txy->jxqy", narrow, records[0], preferred_element_type=jnp.float32
    )

    mine = lax.dynamic_index_in_dim(jnp.asarray(pair), lax.axis_index("freq"), 0, keepdims=False)
    wave = jnp.sum(mine * wavelet, axis=1)
    off = offsets[0].transpose(2, 1, 0)
    off = jnp.pad(off, ((0, 0), (0, 0), (0, LANES - off.shape[2])))
    change = jnp.asarray(basis_change(degrees), jnp.float32)
    tab = jnp.einsum("jk,cfrk->rjfc", change, coefficients, precision=lax.Precision.HIGHEST)
    tab = tab.reshape(2, degrees, group * class_count)
    tab = jnp.pad(tab, ((0, 0), (0, 0), (0, LANES - group * class_count)))

    plane = (2, nx, ny, SUBS, LANES)
    square = pltpu.VMEM((2, LANES, LANES), jnp.float32)
    vmem = pl.BlockSpec(memory_space=pltpu.VMEM)
    smem = pl.BlockSpec(memory_space=pltpu.SMEM)
    return pl.pallas_call(
        functools.partial(migrate_kernel, group, class_count, ranks),
        out_shape=jax.ShapeDtypeStruct((depths, tile_rows, width), jnp.float32),
        in_specs=[vmem, smem, vmem, vmem, vmem],
        out_specs=vmem,
        scratch_shapes=[
            pltpu.VMEM((depths + 1,) + plane, jnp.float32),
            pltpu.VMEM((depths,) + plane[1:], jnp.int32),
            pltpu.VMEM((depths, degrees) + plane, jnp.float32),
            pltpu.VMEM(plane, jnp.float32),
            square,
            square,
            pltpu.VMEM(spectra.shape, jnp.float32),
            pltpu.VMEM((depths, ranks * 16, width), jnp.float32),
            pltpu.VMEM((depths, ranks - 1, 16, width), jnp.float32),
            pltpu.SemaphoreType.DMA,
            pltpu.SemaphoreType.DMA((ranks - 1,)),
            pltpu.SemaphoreType.DMA((ranks - 1,)),
            pltpu.SemaphoreType.DMA((depths, ranks - 1)),
            pltpu.SemaphoreType.DMA((depths, ranks - 1)),
        ],
        compiler_params=pltpu.CompilerParams(
            collective_id=0, has_side_effects=True, vmem_limit_bytes=VMEM_BYTES
        ),
        name="migrate",
    )(off, wave, tab, classes, spectra)


def dft_table(count, record_duration):
    spectral_slots = jnp.arange(count, dtype=jnp.int32) + first_bin
    clock_moments = jnp.arange(record_duration, dtype=jnp.int32)
    elementwise_multiple = spectral_slots[:, None] * clock_moments[None, :] % record_duration
    phase = elementwise_multiple.astype(jnp.float32) * (2.0 * math.pi / record_duration)
    scaling = 1.0 / math.sqrt(record_duration)
    stacked = jnp.stack([jnp.cos(phase), -jnp.sin(phase)], axis=1) * scaling
    return stacked.reshape(2 * count, record_duration)


def mcclellan(field):
    widths = [(0, 0)] * (field.ndim - 2) + [(1, 1), (1, 1)]
    zero_extended = jnp.pad(field, widths)
    along_x = (
        0.25 * zero_extended[..., :-2, :]
        + 0.5 * zero_extended[..., 1:-1, :]
        + 0.25 * zero_extended[..., 2:, :]
    )
    smoothed = 0.25 * along_x[..., :-2] + 0.5 * along_x[..., 1:-1] + 0.25 * along_x[..., 2:]
    return 2.0 * smoothed - field


def add_term(summed_terms, chebyshev, filters, degree):
    wavefield_polarity = jnp.array([1.0, -1.0], jnp.float32)[None, :, None, None, None]
    real_component = filters[:, 0, degree][:, None, None]
    im_part = filters[:, 1, degree][:, None, None] * wavefield_polarity
    cheb_re = chebyshev[:, :, :, 0]
    cheb_im = chebyshev[:, :, :, 1]
    return summed_terms + jnp.stack(
        [
            real_component * cheb_re - im_part * cheb_im,
            real_component * cheb_im + im_part * cheb_re,
        ],
        axis=3,
    )


def extrapolate(fields, filters):
    degrees = filters.shape[2]
    previous = fields
    current = mcclellan(fields)
    summed_terms = add_term(jnp.zeros_like(fields), previous, filters, 0)
    summed_terms = add_term(summed_terms, current, filters, 1)
    for degree in range(2, degrees):
        previous, current = (current, 2.0 * mcclellan(current) - previous)
        summed_terms = add_term(summed_terms, current, filters, degree)
    return summed_terms


def emitter_impulses(offsets, spacing, height, breadth):
    off_x = jnp.repeat(jnp.repeat(offsets[..., 0], spacing, axis=1), spacing, axis=2)
    off_y = jnp.repeat(jnp.repeat(offsets[..., 1], spacing, axis=1), spacing, axis=2)
    row_phase = jnp.arange(height, dtype=jnp.int32) % spacing
    col_phase = jnp.arange(breadth, dtype=jnp.int32) % spacing
    hits = (row_phase[None, :, None] == off_x) & (col_phase[None, None, :] == off_y)
    return hits.astype(jnp.float32)


def plain_device(records, wavelet, offsets, classes, coefficients):
    shot_count, record_duration, tile_rows, width_y = records.shape
    freq_local = coefficients.shape[1]
    fourier_matrix = dft_table(NF, record_duration)
    narrow_table = fourier_matrix.astype(jnp.bfloat16)
    spectra = jnp.stack(
        [
            jnp.dot(
                narrow_table,
                records[0].reshape(record_duration, tile_rows * width_y),
                preferred_element_type=jnp.float32,
            ).reshape(NF, 2, tile_rows, width_y)
        ],
        axis=1,
    )
    receivers = lax.all_to_all(spectra, "freq", split_axis=0, concat_axis=3, tiled=True)
    height = receivers.shape[3]
    wave_spec = (
        jnp.dot(wavelet, fourier_matrix.T, precision=lax.Precision.HIGHEST)
        .reshape(shot_count, NF, 2)
        .transpose(1, 0, 2)
    )
    first_freq = lax.axis_index("freq") * freq_local
    wave_local = lax.dynamic_slice_in_dim(wave_spec, first_freq, freq_local, 0)
    spikes = emitter_impulses(offsets, SPACING, height, width_y)
    source = wave_local[:, :, :, None, None] * spikes[None, :, None]
    fields = jnp.stack([source, receivers], axis=1)
    class_ids = jnp.arange(coefficients.shape[0], dtype=jnp.int32)
    migrated_pictures = []
    for level in range(classes.shape[0]):
        onehot = (classes[level][None] == class_ids[:, None, None]).astype(jnp.float32)
        filters = jnp.einsum(
            "cfrk,cxy->frkxy", coefficients, onehot, precision=lax.Precision.HIGHEST
        )
        fields = extrapolate(fields, filters)
        partial_value = jnp.sum(fields[:, 0] * fields[:, 1], axis=(0, 1, 2))
        migrated_pictures.append(
            lax.psum_scatter(partial_value, "freq", scatter_dimension=0, tiled=True)
        )
    return jnp.stack(migrated_pictures)


def fits_lanes(records, classes, coefficients):
    tile_rows, width = records.shape[2:]
    height = classes.shape[1]
    class_count, group = coefficients.shape[:2]
    return (
        2 * group == SUBS
        and width == LANES
        and width // SUBS == SPACING
        and group * class_count <= LANES
        and height * group % LANES == 0
        and height // tile_rows % 2 == 0
        and 2 * (height * group // LANES) == tile_rows
    )


def per_device(records, wavelet, offsets, classes, coefficients):
    if fits_lanes(records, classes, coefficients):
        return fast_device(records, wavelet, offsets, classes, coefficients)
    return plain_device(records, wavelet, offsets, classes, coefficients)


def solution(mesh):
    placed = (
        P("parts", None, "freq", None),
        P("parts", None),
        P("parts", None, None, None),
        P("parts", None, None),
        P(None, "freq", None, None),
    )
    return jax.shard_map(
        per_device, mesh=mesh, in_specs=placed, out_specs=P("parts", "freq", None), check_vma=False
    )
```

```python
import functools
import math

import jax
import jax.numpy as jnp
import numpy as np
from jax import lax
from jax.experimental import pallas as pl
from jax.experimental.pallas import tpu as pltpu
from jax.sharding import PartitionSpec as P

NF = 64
SPACING = 16
LANES = 128
SUBS = 8
VMEM_BYTES = 60 * 2**20
NODES = (0.75, 1.0)


first_bin = 4


def dft_rows(count, record_duration):
    slots = np.arange(count, dtype=np.int64) + first_bin
    moments = np.arange(record_duration, dtype=np.int64)
    phase = (slots[:, None] * moments[None, :] % record_duration).astype(np.float32)
    phase = phase * np.float32(2.0 * math.pi / record_duration)
    scaling = np.float32(1.0 / math.sqrt(record_duration))
    return np.cos(phase) * scaling, -np.sin(phase) * scaling


def basis_change(degrees):
    poly = np.polynomial.Polynomial
    basis = [poly([1.0])]
    for j in range(degrees - 1):
        node = NODES[j] if j < len(NODES) else 0.0
        basis.append(basis[-1] * poly([-16.0 * node, 16.0]))
    matrix = np.zeros((degrees, degrees))
    for j, b in enumerate(basis):
        matrix[: len(b.coef), j] = b.coef
    out = np.zeros((degrees, degrees))
    for k in range(degrees):
        shifted = np.polynomial.Chebyshev.basis(k).convert(kind=poly)(poly([-1.0, 2.0]))
        coef = np.zeros(degrees)
        coef[: len(shifted.coef)] = shifted.coef
        out[:, k] = np.linalg.solve(matrix, coef)
    return out


def iotas():
    lane = lax.broadcasted_iota(jnp.int32, (SUBS, LANES), 1)
    sub = lax.broadcasted_iota(jnp.int32, (SUBS, LANES), 0)
    return lane, sub


def pick(table, index):
    along_lanes = lax.GatherDimensionNumbers(
        offset_dims=(),
        collapsed_slice_dims=(1,),
        start_index_map=(1,),
        operand_batching_dims=(0,),
        start_indices_batching_dims=(0,),
    )
    return lax.gather(
        table,
        index[..., None],
        along_lanes,
        slice_sizes=(1, 1),
        mode=lax.GatherScatterMode.PROMISE_IN_BOUNDS,
    )


def row_of(tab, part, k):
    return jnp.broadcast_to(tab[k, pl.ds(part, 1), :], (SUBS, LANES))


def lane_classes(classes, idx, flat, group, class_count):
    depths, nx, ny = idx.shape[:3]
    blocks = LANES // group
    lane, _ = iotas()
    places = [(d, x) for d in range(depths) for x in range(nx)]
    for n in range(0, len(places), group):
        some = places[n : n + group]
        rows = [classes[d, pl.ds(x, blocks, stride=nx), :] for d, x in some]
        slot = n // group % 2
        flat[slot] = jnp.transpose(jnp.concatenate(rows, axis=0).astype(jnp.float32))
        for i, (d, x) in enumerate(some):
            for y in range(ny):
                line = flat[slot, pl.ds(y, SUBS, stride=ny), :].astype(jnp.int32)
                idx[d, x, y] = pick(line, lane // group + i * blocks) + lane % group * class_count


def look_up(tab, idx, filters, x, y):
    degrees = tab.shape[0]
    place = idx[x, y]
    for k in range(degrees):
        for part in range(2):
            filters[k, part, x, y] = pick(row_of(tab, part, k), place)


def degree_pass(old, cur, planes, acc, filters, node, group, nx, ny, begin=None, beside=None):
    lane, sub = iotas()
    low, high = lane >= group, lane < LANES - group
    first, last = sub >= 1, sub < SUBS - 1

    def along_x(c, y):
        v = [old[c, x, y] for x in range(nx)]
        before = jnp.where(low, pltpu.roll(v[nx - 1], group, 1), 0.0)
        after = jnp.where(high, pltpu.roll(v[0], LANES - group, 1), 0.0)
        ext = [before] + v + [after]
        pair = [ext[i] + ext[i + 1] for i in range(nx + 1)]
        return [pair[i] + pair[i + 1] for i in range(nx)]

    u, q, u_first = [], [], []
    for c in range(planes):
        end = along_x(c, ny - 1)
        prev = [jnp.where(first, pltpu.roll(e, 1, 0), 0.0) for e in end]
        start = along_x(c, 0)
        u.append(start)
        u_first.append(start)
        q.append([a + b for a, b in zip(prev, start)])
    for y in range(ny):
        made, was = [], []
        for c in range(planes):
            if y < ny - 1:
                nxt = along_x(c, y + 1)
            else:
                nxt = [jnp.where(last, pltpu.roll(e, SUBS - 1, 0), 0.0) for e in u_first[c]]
            q_next = [a + b for a, b in zip(u[c], nxt)]
            total = [a + b for a, b in zip(q[c], q_next)]
            if node is not None:
                held = [old[c, x, y] for x in range(nx)]
                total = [t - node * h for t, h in zip(total, held)]
                was.append(held)
            for x in range(nx):
                cur[c, x, y] = total[x]
            made.append(total)
            u[c], q[c] = nxt, q_next
        for x in range(nx):
            hr, hi = filters[0, x, y], filters[1, x, y]
            if planes == 2:
                re, im = made[0][x], made[1][x]
                if begin is None:
                    acc[0, x, y] = acc[0, x, y] + (hr * re - hi * im)
                    acc[1, x, y] = acc[1, x, y] + (hr * im + hi * re)
                else:
                    gr, gi = begin[0, x, y], begin[1, x, y]
                    was_re, was_im = was[0][x], was[1][x]
                    acc[0, x, y] = (gr * was_re - gi * was_im) + (hr * re - hi * im)
                    acc[1, x, y] = (gr * was_im + gi * was_re) + (hr * im + hi * re)
            else:
                acc[0, x, y] = acc[0, x, y] + hr * made[0][x]
                acc[1, x, y] = acc[1, x, y] + hi * made[0][x]
        if beside is not None:
            beside(y)


def node_at(j):
    node = jnp.float32(16.0 * NODES[-1])
    for n, value in enumerate(NODES[:-1]):
        node = jnp.where(j == n, jnp.float32(16.0 * value), node)
    return node


def spread_ahead(ahead, steps, j, nx, ny):
    if ahead is None:
        return None
    share = nx * ny // steps

    def beside(y):
        for n in range(share * y // ny, share * (y + 1) // ny):
            ahead(n % nx, j * (share // nx) + n // nx)

    return beside


def all_degrees(cur, planes, acc, filters, group, nx, ny, ahead=None, begin=None):
    steps = filters.shape[0] - 1
    done = 0
    if begin is not None:
        degree_pass(
            begin, cur, planes, acc, filters.at[1], 16.0 * NODES[0], group, nx, ny,
            filters.at[0], spread_ahead(ahead, steps, 0, nx, ny),
        )
        done = 1

    def one(shifted, j, carry):
        degree_pass(
            cur, cur, planes, acc, filters.at[j + 1], node_at(j) if shifted else None,
            group, nx, ny, None, spread_ahead(ahead, steps, j, nx, ny),
        )
        return carry

    if len(NODES) - done == 1:
        one(True, done, 0)
    else:
        lax.fori_loop(done, len(NODES), functools.partial(one, True), 0)
    lax.fori_loop(len(NODES), steps, functools.partial(one, False), 0)


def source_steps(group, off_ref, wave, tab, out, idx, filters, cur):
    depths, nx, ny = idx.shape[:3]
    lane, _ = iotas()

    row_x = [lane // group * nx + x for x in range(nx)]
    off_x = [pick(off_ref[0], r // SPACING) for r in row_x]
    off_y = [pick(off_ref[1], r // SPACING) for r in row_x]

    def spike_row(y, carry):
        for x in range(nx):
            hit = (row_x[x] % SPACING == off_x[x]) & (off_y[x] == y)
            v = jnp.where(hit, 1.0, 0.0)
            cur[0, x, y] = v
            out[0, 0, x, y] = filters[0, 0, 0, x, y] * v
            out[0, 1, x, y] = filters[0, 0, 1, x, y] * v
        return carry

    lax.fori_loop(0, ny, spike_row, 0, unroll=2)

    def ahead_of(d):
        return functools.partial(look_up, tab, idx.at[d], filters.at[d])

    all_degrees(cur, 1, out.at[0], filters.at[0], group, nx, ny, ahead_of(1))
    wr, wi = jnp.zeros((SUBS, LANES), jnp.float32), jnp.zeros((SUBS, LANES), jnp.float32)
    for f in range(group):
        wr = jnp.where(lane % group == f, jnp.broadcast_to(wave[pl.ds(f, 1), :], wr.shape), wr)
        wi = jnp.where(
            lane % group == f, -jnp.broadcast_to(wave[pl.ds(group + f, 1), :], wi.shape), wi
        )

    def wave_row(y, carry):
        for x in range(nx):
            re, im = out[0, 0, x, y], out[0, 1, x, y]
            out[0, 0, x, y] = wr * re - wi * im
            out[0, 1, x, y] = wr * im + wi * re
        return carry

    lax.fori_loop(0, ny, wave_row, 0, unroll=2)

    def depth(d, carry):
        filter_step(group, cur, out.at[d - 1], out.at[d], filters.at[d], ahead_of(d + 1))
        return carry

    lax.fori_loop(1, depths - 1, depth, 0)


def filter_step(group, cur, begin, end, filters, ahead=None):
    nx, ny = begin.shape[1:3]
    all_degrees(cur, 2, end, filters, group, nx, ny, ahead, begin)


def small_tables(offsets, wavelet, coefs, off, wave, tab, wide, moments):
    group, degrees, _, class_count = coefs.shape
    rows, columns = offsets.shape[0], offsets.shape[2]
    for by in range(rows):
        for c in range(2):
            off[c, pl.ds(by, 1), pl.ds(0, columns)] = offsets[by, pl.ds(c, 1), :]
    wave[...] = jnp.broadcast_to(
        jnp.sum(moments[...] * wavelet[...], axis=1, keepdims=True), wave.shape
    )
    wide[...] = jnp.zeros_like(wide)
    for f in range(group):
        for k in range(degrees):
            wide[f, k, pl.ds(0, 2), pl.ds(0, class_count)] = coefs[f, k]
    joined = []
    for k in range(degrees):
        row = wide[0, k]
        for f in range(1, group):
            row = row + pltpu.roll(wide[f, k], f * class_count, 1)
        joined.append(row)
    change = basis_change(degrees)
    for j in range(degrees):
        total = None
        for k in range(degrees):
            if change[j, k] != 0.0:
                term = np.float32(change[j, k]) * joined[k]
                total = term if total is None else total + term
        tab[j] = total


def exchange_peers(ranks):
    me = lax.axis_index("freq")
    return me, [lax.rem(me + k, ranks) for k in range(1, ranks)]


def remote(src, dst, send, recv, peer):
    return pltpu.make_async_remote_copy(
        src_ref=src,
        dst_ref=dst,
        send_sem=send,
        recv_sem=recv,
        device_id={"freq": peer},
        device_id_type=pl.DeviceIdType.MESH,
    )


def unpack_received(received, acc, flat, group, nx, ny):
    senders = received.shape[0]
    sub3 = lax.broadcasted_iota(jnp.int32, (senders, SUBS, LANES), 1)
    upper = sub3 < group
    for x in range(nx):
        a, b = received[:, x], received[:, nx + x]
        parts = (
            jnp.where(upper, a, pltpu.roll(b, group, 1)),
            jnp.where(upper, pltpu.roll(a, group, 1), b),
        )
        for r in range(2):
            flat[r] = jnp.transpose(parts[r].reshape(LANES, LANES))
            for y in range(ny):
                acc[r, x, y] = flat[r, pl.ds(y, SUBS, stride=ny), :]


def form_image(src, acc, flat, turned, image, group, nx, ny):
    owners = image.shape[0] // 16
    for x in range(nx):
        for y in range(ny):
            v = src[0, x, y] * acc[0, x, y] - src[1, x, y] * acc[1, x, y]
            flat[x % 2, pl.ds(y, SUBS, stride=ny), :] = v
        turned[x % 2] = jnp.transpose(flat[x % 2])
        for b in range(2):
            total = turned[x % 2, pl.ds(b * group, owners, stride=2 * group), :]
            for f in range(1, group):
                total = total + turned[x % 2, pl.ds(b * group + f, owners, stride=2 * group), :]
            image[pl.ds(b * nx + x, owners, stride=16), :] = total


def migrate_kernel(
    group, class_count, ranks,
    records, table, moments_all, wavelet, offsets, coefs, classes,
    out,
    fields, idx, filters, cur, flat, turned, received, image, slots,
    traces, spectra, moments, off, wave, wide, tab,
    local_sem, rec_sem, a_send, a_recv, i_send, i_recv,
):
    depths, nx, ny = idx.shape[:3]
    tile = records.shape[0]
    halves, pairs = 2, tile // 4
    me, peers = exchange_peers(ranks)
    barrier = pltpu.get_barrier_semaphore()
    for peer in peers:
        pl.semaphore_signal(
            barrier, inc=1, device_id={"freq": peer}, device_id_type=pl.DeviceIdType.MESH
        )
    mine = pltpu.make_async_copy(moments_all.at[me], moments, local_sem)
    mine.start()

    def load(p):
        rows = pl.ds(2 * p, 2)
        return pltpu.make_async_copy(records.at[rows], traces.at[rows], rec_sem.at[p])

    for p in range(halves * pairs):
        load(p).start()
    mine.wait()
    small_tables(offsets, wavelet, coefs, off, wave, tab, wide, moments)
    lane_classes(classes, idx, flat, group, class_count)
    pl.semaphore_wait(barrier, ranks - 1)

    def spread(half):
        rows = pl.ds(half * 2 * pairs, 2 * pairs)
        return [
            remote(
                spectra.at[peer, rows],
                received.at[me, rows],
                a_send.at[half, k],
                a_recv.at[half, k],
                peer,
            )
            for k, peer in enumerate(peers)
        ]

    def transform(half, carry):
        def pair(i, carry):
            p = half * pairs + i
            load(p).wait()
            both = jnp.concatenate([traces[2 * p], traces[2 * p + 1]], axis=1)
            made = jnp.dot(table[...], both, preferred_element_type=jnp.float32)
            width = made.shape[1] // 2
            for n in range(2):
                spectra[:, 2 * p + n] = made[:, n * width : (n + 1) * width].reshape(
                    ranks, SUBS, width
                )
            share = nx * ny // (halves * pairs)
            for n in range(share):
                at = p * share + n
                look_up(tab, idx.at[0], filters.at[0], at // ny, at % ny)
            return carry

        lax.fori_loop(0, pairs, pair, 0)
        for copy in spread(half):
            copy.start()
        return carry

    lax.fori_loop(0, halves, transform, 0)
    own = pltpu.make_async_copy(spectra.at[me], received.at[me], local_sem)
    own.start()
    source_steps(group, off, wave, tab, fields, idx, filters, cur)
    acc = fields.at[depths]

    def sends(d):
        return [
            remote(
                image.at[d, pl.ds(peer * 16, 16)],
                slots.at[d, k],
                i_send.at[d, k],
                i_recv.at[d, k],
                peer,
            )
            for k, peer in enumerate(peers)
        ]

    def step(n, carry):
        @pl.when(n == 1)
        def _():
            own.wait()
            for half in range(halves):
                for copy in spread(half):
                    copy.wait()
            unpack_received(received, acc, flat, group, nx, ny)

        ready = jnp.minimum(n, 1)
        begin = (depths - 2) * (1 - ready) + depths * ready
        end = depths - 1 + ready
        d = (depths - 1) * (1 - ready) + (n - 1) * ready
        filter_step(group, cur, fields.at[begin], fields.at[end], filters.at[d])

        @pl.when(n >= 1)
        def _():
            form_image(fields.at[d], acc, flat, turned, image.at[d], group, nx, ny)
            for copy in sends(d):
                copy.start()

        return carry

    lax.fori_loop(0, depths + 1, step, 0)
    for d in range(depths):
        total = image[d, pl.ds(me * 16, 16), :]
        for k, copy in enumerate(sends(d)):
            copy.wait_recv()
            total = total + slots[d, k]
        out[d] = total[:tile]
    for d in range(depths):
        for copy in sends(d):
            copy.wait_send()


def fast_device(records, wavelet, offsets, classes, coefficients):
    _, record_duration, tile_rows, width = records.shape
    depths, height, _ = classes.shape
    class_count, group, _, degrees = coefficients.shape
    ranks = height // tile_rows
    nx, ny = group * height // LANES, width // SUBS
    cos_rows, sin_rows = dft_rows(NF, record_duration)
    pair = np.stack(
        [cos_rows.reshape(ranks, group, -1), -sin_rows.reshape(ranks, group, -1)], axis=1
    ).reshape(ranks, 2 * group, record_duration)
    narrow = jnp.asarray(pair.reshape(2 * NF, record_duration)).astype(jnp.bfloat16)
    plane = (2, nx, ny, SUBS, LANES)
    square = pltpu.VMEM((2, LANES, LANES), jnp.float32)
    vmem = pl.BlockSpec(memory_space=pltpu.VMEM)
    hbm = pl.BlockSpec(memory_space=pl.ANY)
    return pl.pallas_call(
        functools.partial(migrate_kernel, group, class_count, ranks),
        out_shape=jax.ShapeDtypeStruct((depths, tile_rows, width), jnp.float32),
        in_specs=[hbm, vmem, hbm, vmem, vmem, vmem, vmem],
        out_specs=vmem,
        scratch_shapes=[
            pltpu.VMEM((depths + 1,) + plane, jnp.float32),
            pltpu.VMEM((depths,) + plane[1:], jnp.int32),
            pltpu.VMEM((depths, degrees) + plane, jnp.float32),
            pltpu.VMEM(plane, jnp.float32),
            square,
            square,
            pltpu.VMEM((ranks, tile_rows, SUBS, width), jnp.float32),
            pltpu.VMEM((depths, ranks * 16, width), jnp.float32),
            pltpu.VMEM((depths, ranks - 1, 16, width), jnp.float32),
            pltpu.VMEM((tile_rows, record_duration, width), jnp.bfloat16),
            pltpu.VMEM((ranks, tile_rows, SUBS, width), jnp.float32),
            pltpu.VMEM((2 * group, record_duration), jnp.float32),
            pltpu.VMEM((2, SUBS, LANES), jnp.int32),
            pltpu.VMEM((SUBS, LANES), jnp.float32),
            pltpu.VMEM((group, degrees, SUBS, LANES), jnp.float32),
            pltpu.VMEM((degrees, SUBS, LANES), jnp.float32),
            pltpu.SemaphoreType.DMA,
            pltpu.SemaphoreType.DMA((tile_rows // 2,)),
            pltpu.SemaphoreType.DMA((2, ranks - 1)),
            pltpu.SemaphoreType.DMA((2, ranks - 1)),
            pltpu.SemaphoreType.DMA((depths, ranks - 1)),
            pltpu.SemaphoreType.DMA((depths, ranks - 1)),
        ],
        compiler_params=pltpu.CompilerParams(
            collective_id=0, has_side_effects=True, vmem_limit_bytes=VMEM_BYTES
        ),
        name="migrate",
    )(
        records[0].transpose(1, 0, 2),
        narrow,
        jnp.asarray(pair),
        wavelet,
        offsets[0].transpose(1, 2, 0),
        coefficients.transpose(1, 3, 2, 0),
        classes,
    )


def dft_table(count, record_duration):
    spectral_slots = jnp.arange(count, dtype=jnp.int32) + first_bin
    clock_moments = jnp.arange(record_duration, dtype=jnp.int32)
    elementwise_multiple = spectral_slots[:, None] * clock_moments[None, :] % record_duration
    phase = elementwise_multiple.astype(jnp.float32) * (2.0 * math.pi / record_duration)
    scaling = 1.0 / math.sqrt(record_duration)
    stacked = jnp.stack([jnp.cos(phase), -jnp.sin(phase)], axis=1) * scaling
    return stacked.reshape(2 * count, record_duration)


def mcclellan(field):
    widths = [(0, 0)] * (field.ndim - 2) + [(1, 1), (1, 1)]
    zero_extended = jnp.pad(field, widths)
    along_x = (
        0.25 * zero_extended[..., :-2, :]
        + 0.5 * zero_extended[..., 1:-1, :]
        + 0.25 * zero_extended[..., 2:, :]
    )
    smoothed = 0.25 * along_x[..., :-2] + 0.5 * along_x[..., 1:-1] + 0.25 * along_x[..., 2:]
    return 2.0 * smoothed - field


def add_term(summed_terms, chebyshev, filters, degree):
    wavefield_polarity = jnp.array([1.0, -1.0], jnp.float32)[None, :, None, None, None]
    real_component = filters[:, 0, degree][:, None, None]
    im_part = filters[:, 1, degree][:, None, None] * wavefield_polarity
    cheb_re = chebyshev[:, :, :, 0]
    cheb_im = chebyshev[:, :, :, 1]
    return summed_terms + jnp.stack(
        [
            real_component * cheb_re - im_part * cheb_im,
            real_component * cheb_im + im_part * cheb_re,
        ],
        axis=3,
    )


def extrapolate(fields, filters):
    degrees = filters.shape[2]
    previous = fields
    current = mcclellan(fields)
    summed_terms = add_term(jnp.zeros_like(fields), previous, filters, 0)
    summed_terms = add_term(summed_terms, current, filters, 1)
    for degree in range(2, degrees):
        previous, current = (current, 2.0 * mcclellan(current) - previous)
        summed_terms = add_term(summed_terms, current, filters, degree)
    return summed_terms


def emitter_impulses(offsets, spacing, height, breadth):
    off_x = jnp.repeat(jnp.repeat(offsets[..., 0], spacing, axis=1), spacing, axis=2)
    off_y = jnp.repeat(jnp.repeat(offsets[..., 1], spacing, axis=1), spacing, axis=2)
    row_phase = jnp.arange(height, dtype=jnp.int32) % spacing
    col_phase = jnp.arange(breadth, dtype=jnp.int32) % spacing
    hits = (row_phase[None, :, None] == off_x) & (col_phase[None, None, :] == off_y)
    return hits.astype(jnp.float32)


def plain_device(records, wavelet, offsets, classes, coefficients):
    shot_count, record_duration, tile_rows, width_y = records.shape
    freq_local = coefficients.shape[1]
    fourier_matrix = dft_table(NF, record_duration)
    narrow_table = fourier_matrix.astype(jnp.bfloat16)
    spectra = jnp.stack(
        [
            jnp.dot(
                narrow_table,
                records[0].reshape(record_duration, tile_rows * width_y),
                preferred_element_type=jnp.float32,
            ).reshape(NF, 2, tile_rows, width_y)
        ],
        axis=1,
    )
    receivers = lax.all_to_all(spectra, "freq", split_axis=0, concat_axis=3, tiled=True)
    height = receivers.shape[3]
    wave_spec = (
        jnp.dot(wavelet, fourier_matrix.T, precision=lax.Precision.HIGHEST)
        .reshape(shot_count, NF, 2)
        .transpose(1, 0, 2)
    )
    first_freq = lax.axis_index("freq") * freq_local
    wave_local = lax.dynamic_slice_in_dim(wave_spec, first_freq, freq_local, 0)
    spikes = emitter_impulses(offsets, SPACING, height, width_y)
    source = wave_local[:, :, :, None, None] * spikes[None, :, None]
    fields = jnp.stack([source, receivers], axis=1)
    class_ids = jnp.arange(coefficients.shape[0], dtype=jnp.int32)
    migrated_pictures = []
    for level in range(classes.shape[0]):
        onehot = (classes[level][None] == class_ids[:, None, None]).astype(jnp.float32)
        filters = jnp.einsum(
            "cfrk,cxy->frkxy", coefficients, onehot, precision=lax.Precision.HIGHEST
        )
        fields = extrapolate(fields, filters)
        partial_value = jnp.sum(fields[:, 0] * fields[:, 1], axis=(0, 1, 2))
        migrated_pictures.append(
            lax.psum_scatter(partial_value, "freq", scatter_dimension=0, tiled=True)
        )
    return jnp.stack(migrated_pictures)


def fits_lanes(records, classes, coefficients):
    tile_rows, width = records.shape[2:]
    height = classes.shape[1]
    class_count, group = coefficients.shape[:2]
    return (
        2 * group == SUBS
        and width == LANES
        and width // SUBS == SPACING
        and group * class_count <= LANES
        and height * group % LANES == 0
        and height // tile_rows % 2 == 0
        and 2 * (height * group // LANES) == tile_rows
    )


def per_device(records, wavelet, offsets, classes, coefficients):
    if fits_lanes(records, classes, coefficients):
        return fast_device(records, wavelet, offsets, classes, coefficients)
    return plain_device(records, wavelet, offsets, classes, coefficients)


def solution(mesh):
    placed = (
        P("parts", None, "freq", None),
        P("parts", None),
        P("parts", None, None, None),
        P("parts", None, None),
        P(None, "freq", None, None),
    )
    return jax.shard_map(
        per_device, mesh=mesh, in_specs=placed, out_specs=P("parts", "freq", None), check_vma=False
    )
```

```python
import functools
import math

import jax
import jax.numpy as jnp
import numpy as np
from jax import lax
from jax.experimental import pallas as pl
from jax.experimental.pallas import tpu as pltpu
from jax.sharding import PartitionSpec as P

NF = 64
SPACING = 16
LANES = 128
SUBS = 8
VMEM_BYTES = 60 * 2**20
NODES = (0.75, 1.0)


first_bin = 4


def dft_rows(count, record_duration):
    slots = np.arange(count, dtype=np.int64) + first_bin
    moments = np.arange(record_duration, dtype=np.int64)
    phase = (slots[:, None] * moments[None, :] % record_duration).astype(np.float32)
    phase = phase * np.float32(2.0 * math.pi / record_duration)
    scaling = np.float32(1.0 / math.sqrt(record_duration))
    return np.cos(phase) * scaling, -np.sin(phase) * scaling


def basis_change(degrees):
    poly = np.polynomial.Polynomial
    basis = [poly([1.0])]
    for j in range(degrees - 1):
        node = NODES[j] if j < len(NODES) else 0.0
        basis.append(basis[-1] * poly([-16.0 * node, 16.0]))
    matrix = np.zeros((degrees, degrees))
    for j, b in enumerate(basis):
        matrix[: len(b.coef), j] = b.coef
    out = np.zeros((degrees, degrees))
    for k in range(degrees):
        shifted = np.polynomial.Chebyshev.basis(k).convert(kind=poly)(poly([-1.0, 2.0]))
        coef = np.zeros(degrees)
        coef[: len(shifted.coef)] = shifted.coef
        out[:, k] = np.linalg.solve(matrix, coef)
    return out


def iotas():
    lane = lax.broadcasted_iota(jnp.int32, (SUBS, LANES), 1)
    sub = lax.broadcasted_iota(jnp.int32, (SUBS, LANES), 0)
    return lane, sub


def pick(table, index):
    along_lanes = lax.GatherDimensionNumbers(
        offset_dims=(),
        collapsed_slice_dims=(1,),
        start_index_map=(1,),
        operand_batching_dims=(0,),
        start_indices_batching_dims=(0,),
    )
    return lax.gather(
        table,
        index[..., None],
        along_lanes,
        slice_sizes=(1, 1),
        mode=lax.GatherScatterMode.PROMISE_IN_BOUNDS,
    )


def row_of(tab, part, k):
    return jnp.broadcast_to(tab[k, pl.ds(part, 1), :], (SUBS, LANES))


def lane_classes(classes, idx, flat, group, class_count):
    depths, nx, ny = idx.shape[:3]
    blocks = LANES // group
    lane, _ = iotas()
    places = [(d, x) for d in range(depths) for x in range(nx)]
    for n in range(0, len(places), group):
        some = places[n : n + group]
        rows = [classes[d, pl.ds(x, blocks, stride=nx), :] for d, x in some]
        slot = n // group
        flat[slot] = jnp.transpose(jnp.concatenate(rows, axis=0).astype(jnp.float32))
        for i, (d, x) in enumerate(some):
            for y in range(ny):
                line = flat[slot, pl.ds(y, SUBS, stride=ny), :].astype(jnp.int32)
                idx[d, x, y] = pick(line, lane // group + i * blocks) + lane % group * class_count


def look_up(tab, idx, store, x, y):
    place = idx[x, y]
    for k in range(tab.shape[0]):
        for part in range(2):
            store(k, part, pick(row_of(tab, part, k), place))


def planes_at(filters, x, y):
    def store(k, part, value):
        filters[k, part, x, y] = value

    return store


def degree_pass(old, cur, planes, acc, filters, node, group, nx, ny, begin=None, beside=None, kept=None):
    lane, sub = iotas()
    low, high = lane >= group, lane < LANES - group
    first, last = sub >= 1, sub < SUBS - 1

    def along_x(c, y):
        v = [old[c, x, y] for x in range(nx)]
        before = jnp.where(low, pltpu.roll(v[nx - 1], group, 1), 0.0)
        after = jnp.where(high, pltpu.roll(v[0], LANES - group, 1), 0.0)
        ext = [before] + v + [after]
        pair = [ext[i] + ext[i + 1] for i in range(nx + 1)]
        return [pair[i] + pair[i + 1] for i in range(nx)]

    u, q, u_first = [], [], []
    for c in range(planes):
        end = along_x(c, ny - 1)
        prev = [jnp.where(first, pltpu.roll(e, 1, 0), 0.0) for e in end]
        start = along_x(c, 0)
        u.append(start)
        u_first.append(start)
        q.append([a + b for a, b in zip(prev, start)])
    for y in range(ny):
        made, was = [], []
        for c in range(planes):
            if y < ny - 1:
                nxt = along_x(c, y + 1)
            else:
                nxt = [jnp.where(last, pltpu.roll(e, SUBS - 1, 0), 0.0) for e in u_first[c]]
            q_next = [a + b for a, b in zip(u[c], nxt)]
            total = [a + b for a, b in zip(q[c], q_next)]
            if node is not None:
                held = [old[c, x, y] for x in range(nx)]
                total = [t - node * h for t, h in zip(total, held)]
                was.append(held)
                if kept is not None:
                    for x in range(nx):
                        kept[c, x, y] = held[x]
            for x in range(nx):
                cur[c, x, y] = total[x]
            made.append(total)
            u[c], q[c] = nxt, q_next
        for x in range(nx):
            hr, hi = filters[0, x, y], filters[1, x, y]
            if planes == 2:
                re, im = made[0][x], made[1][x]
                if begin is None:
                    acc[0, x, y] = acc[0, x, y] + (hr * re - hi * im)
                    acc[1, x, y] = acc[1, x, y] + (hr * im + hi * re)
                else:
                    gr, gi = begin[0, x, y], begin[1, x, y]
                    was_re, was_im = was[0][x], was[1][x]
                    acc[0, x, y] = (gr * was_re - gi * was_im) + (hr * re - hi * im)
                    acc[1, x, y] = (gr * was_im + gi * was_re) + (hr * im + hi * re)
            else:
                acc[0, x, y] = acc[0, x, y] + hr * made[0][x]
                acc[1, x, y] = acc[1, x, y] + hi * made[0][x]
        if beside is not None:
            beside(y)


def node_at(j):
    node = jnp.float32(16.0 * NODES[-1])
    for n, value in enumerate(NODES[:-1]):
        node = jnp.where(j == n, jnp.float32(16.0 * value), node)
    return node


def spread_ahead(ahead, steps, j, nx, ny):
    if ahead is None:
        return None
    tab, idx, filters, staged = ahead
    share, slots = nx * ny // steps, 0 if staged is None else staged.shape[0]

    def at(n):
        return n % nx, j * (share // nx) + n // nx

    def flush(n):
        for k in range(tab.shape[0]):
            for part in range(2):
                filters[(k, part) + at(n)] = staged[n % slots, k, part]

    def beside(y):
        for n in range(share * y // ny, share * (y + 1) // ny):
            if staged is None:
                look_up(tab, idx, planes_at(filters, *at(n)), *at(n))
                continue
            if n >= slots:
                flush(n - slots)

            def store(k, part, value):
                staged[n % slots, k, part] = value

            look_up(tab, idx, store, *at(n))
        if y == ny - 1 and staged is not None:
            for n in range(share - slots, share):
                flush(n)

    return beside


def all_degrees(cur, planes, acc, filters, group, nx, ny, ahead=None, fresh=False, kept=None):
    steps = filters.shape[0] - 1
    def one(shifted, j, carry):
        degree_pass(
            cur, cur, planes, acc, filters.at[j + 1], node_at(j) if shifted else None,
            group, nx, ny, None, spread_ahead(ahead, steps, j, nx, ny),
        )
        return carry

    done = 0
    if fresh:
        degree_pass(
            acc, cur, planes, acc, filters.at[1], 16.0 * NODES[0], group, nx, ny,
            filters.at[0], spread_ahead(ahead, steps, 0, nx, ny), kept,
        )
        one(True, 1, 0)
    else:
        lax.fori_loop(0, len(NODES), functools.partial(one, True), 0)
    lax.fori_loop(len(NODES), steps, functools.partial(one, False), 0)


def source_steps(group, off_ref, wave, tab, out, kept, idx, filters, cur, staged):
    depths, nx, ny = idx.shape[:3]
    lane, _ = iotas()

    row_x = [lane // group * nx + x for x in range(nx)]
    off_x = [pick(off_ref[0], r // SPACING) for r in row_x]
    off_y = [pick(off_ref[1], r // SPACING) for r in row_x]

    def spike_row(y, carry):
        for x in range(nx):
            hit = (row_x[x] % SPACING == off_x[x]) & (off_y[x] == y)
            v = jnp.where(hit, 1.0, 0.0)
            cur[0, x, y] = v
            out[0, x, y] = filters[0, 0, 0, x, y] * v
            out[1, x, y] = filters[0, 0, 1, x, y] * v
        return carry

    lax.fori_loop(0, ny, spike_row, 0, unroll=2)

    def ahead_of(d, staged=None):
        return tab, idx.at[d], filters.at[d], staged

    all_degrees(cur, 1, out, filters.at[0], group, nx, ny, ahead_of(1))
    wr, wi = jnp.zeros((SUBS, LANES), jnp.float32), jnp.zeros((SUBS, LANES), jnp.float32)
    for f in range(group):
        wr = jnp.where(lane % group == f, jnp.broadcast_to(wave[pl.ds(f, 1), :], wr.shape), wr)
        wi = jnp.where(
            lane % group == f, -jnp.broadcast_to(wave[pl.ds(group + f, 1), :], wi.shape), wi
        )

    def wave_row(y, carry):
        for x in range(nx):
            re, im = out[0, x, y], out[1, x, y]
            out[0, x, y] = wr * re - wi * im
            out[1, x, y] = wr * im + wi * re
        return carry

    lax.fori_loop(0, ny, wave_row, 0, unroll=2)

    def depth(d, carry):
        filter_step(group, cur, out, filters.at[d], kept.at[d - 1], ahead_of(d + 1))
        return carry

    lax.fori_loop(1, depths - 1, depth, 0)


def filter_step(group, cur, field, filters, kept, ahead=None):
    nx, ny = field.shape[1:3]
    all_degrees(cur, 2, field, filters, group, nx, ny, ahead, True, kept)


def small_tables(offsets, wavelet, coefs, off, wave, tab, wide, moments):
    group, degrees, _, class_count = coefs.shape
    rows, columns = offsets.shape[0], offsets.shape[2]
    for by in range(rows):
        for c in range(2):
            off[c, pl.ds(by, 1), pl.ds(0, columns)] = offsets[by, pl.ds(c, 1), :]
    wave[...] = jnp.broadcast_to(
        jnp.sum(moments[...] * wavelet[...], axis=1, keepdims=True), wave.shape
    )
    wide[...] = jnp.zeros_like(wide)
    for f in range(group):
        for k in range(degrees):
            wide[f, k, pl.ds(0, 2), pl.ds(0, class_count)] = coefs[f, k]
    joined = []
    for k in range(degrees):
        row = wide[0, k]
        for f in range(1, group):
            row = row + pltpu.roll(wide[f, k], f * class_count, 1)
        joined.append(row)
    change = basis_change(degrees)
    for j in range(degrees):
        total = None
        for k in range(degrees):
            if change[j, k] != 0.0:
                term = np.float32(change[j, k]) * joined[k]
                total = term if total is None else total + term
        tab[j] = total


def exchange_peers(ranks):
    me = lax.axis_index("freq")
    return me, [lax.rem(me + k, ranks) for k in range(1, ranks)]


def remote(src, dst, send, recv, peer):
    return pltpu.make_async_remote_copy(
        src_ref=src,
        dst_ref=dst,
        send_sem=send,
        recv_sem=recv,
        device_id={"freq": peer},
        device_id_type=pl.DeviceIdType.MESH,
    )


def unpack_received(received, acc, flat, group, nx, ny):
    senders = received.shape[0]
    sub3 = lax.broadcasted_iota(jnp.int32, (senders, SUBS, LANES), 1)
    upper = sub3 < group
    for x in range(nx):
        a, b = received[:, x], received[:, nx + x]
        parts = (
            jnp.where(upper, a, pltpu.roll(b, group, 1)),
            jnp.where(upper, pltpu.roll(a, group, 1), b),
        )
        for r in range(2):
            flat[r] = jnp.transpose(parts[r].reshape(LANES, LANES))
            for y in range(ny):
                acc[r, x, y] = flat[r, pl.ds(y, SUBS, stride=ny), :]


def form_image(src, acc, flat, turned, image, group, nx, ny):
    owners = image.shape[0] // 16
    for x in range(nx):
        for y in range(ny):
            v = src[0, x, y] * acc[0, x, y] - src[1, x, y] * acc[1, x, y]
            flat[x, pl.ds(y, SUBS, stride=ny), :] = v
        turned[x] = jnp.transpose(flat[x])
        for b in range(2):
            total = turned[x, pl.ds(b * group, owners, stride=2 * group), :]
            for f in range(1, group):
                total = total + turned[x, pl.ds(b * group + f, owners, stride=2 * group), :]
            image[pl.ds(b * nx + x, owners, stride=16), :] = total


def migrate_kernel(
    group, class_count, ranks,
    records, table, moments_all, wavelet, offsets, coefs, classes,
    near, rest,
    fields, kept, idx, filters, staged, cur, flat, turned, received, image, slots,
    traces, spectra, moments, off, wave, wide, tab,
    local_sem, rec_sem, a_send, a_recv, i_send, i_recv,
):
    depths, nx, ny = idx.shape[:3]
    tile = records.shape[0]
    halves, pairs = 2, tile // 4
    me, peers = exchange_peers(ranks)
    barrier = pltpu.get_barrier_semaphore()
    for peer in peers:
        pl.semaphore_signal(
            barrier, inc=1, device_id={"freq": peer}, device_id_type=pl.DeviceIdType.MESH
        )
    mine = pltpu.make_async_copy(moments_all.at[me], moments, local_sem)
    mine.start()

    def load(p):
        rows = pl.ds(2 * p, 2)
        return pltpu.make_async_copy(records.at[rows], traces.at[rows], rec_sem.at[p])

    for p in range(halves * pairs):
        load(p).start()
    mine.wait()
    small_tables(offsets, wavelet, coefs, off, wave, tab, wide, moments)
    lane_classes(classes, idx, flat, group, class_count)
    pl.semaphore_wait(barrier, ranks - 1)

    def spread(half):
        rows = pl.ds(half * 2 * pairs, 2 * pairs)
        return [
            remote(
                spectra.at[peer, rows],
                received.at[me, rows],
                a_send.at[half, k],
                a_recv.at[half, k],
                peer,
            )
            for k, peer in enumerate(peers)
        ]

    def transform(half, carry):
        def pair(i, carry):
            p = half * pairs + i
            load(p).wait()
            both = jnp.concatenate([traces[2 * p], traces[2 * p + 1]], axis=1)
            made = jnp.dot(table[...], both, preferred_element_type=jnp.float32)
            width = made.shape[1] // 2
            for n in range(2):
                spectra[:, 2 * p + n] = made[:, n * width : (n + 1) * width].reshape(
                    ranks, SUBS, width
                )
            share = nx * ny // (halves * pairs)
            for n in range(share):
                at = p * share + n
                look_up(tab, idx.at[0], planes_at(filters.at[0], at // ny, at % ny), at // ny, at % ny)
            return carry

        lax.fori_loop(0, pairs, pair, 0)
        for copy in spread(half):
            copy.start()
        return carry

    lax.fori_loop(0, halves, transform, 0)
    own = pltpu.make_async_copy(spectra.at[me], received.at[me], local_sem)
    own.start()
    source_steps(group, off, wave, tab, fields.at[0], kept, idx, filters, cur, staged)
    acc = fields.at[1]

    def sends(d):
        return [
            remote(
                image.at[d, pl.ds(peer * 16, tile)],
                slots.at[d, k],
                i_send.at[d, k],
                i_recv.at[d, k],
                peer,
            )
            for k, peer in enumerate(peers)
        ]

    def step(n, carry):
        @pl.when(n == 1)
        def _():
            own.wait()
            for half in range(halves):
                for copy in spread(half):
                    copy.wait()
            kept[depths - 1] = fields[0]
            unpack_received(received, acc, flat, group, nx, ny)

        ready = jnp.minimum(n, 1)
        d = (depths - 1) * (1 - ready) + (n - 1) * ready
        spare = (depths - 2) * (1 - ready) + depths * ready
        filter_step(group, cur, fields.at[ready], filters.at[d], kept.at[spare])

        @pl.when(n >= 1)
        def _():
            form_image(kept.at[d], acc, flat, turned, image.at[d], group, nx, ny)
            for copy in sends(d):
                copy.start()

        return carry

    lax.fori_loop(0, depths + 1, step, 0)
    for d in range(depths):
        copies = sends(d)
        for copy in copies:
            copy.wait_send()
        sums = [image[d, pl.ds(me * 16, tile), :], None]
        for k, copy in enumerate(copies):
            copy.wait_recv()
            n = k * 2 // ranks
            sums[n] = slots[d, k] if sums[n] is None else sums[n] + slots[d, k]
        near[:, d, :] = sums[0]
        rest[:, d, :] = sums[1]


def fast_device(records, wavelet, offsets, classes, coefficients):
    _, record_duration, tile_rows, width = records.shape
    depths, height, _ = classes.shape
    class_count, group, _, degrees = coefficients.shape
    ranks = height // tile_rows
    nx, ny = group * height // LANES, width // SUBS
    cos_rows, sin_rows = dft_rows(NF, record_duration)
    pair = np.stack(
        [cos_rows.reshape(ranks, group, -1), -sin_rows.reshape(ranks, group, -1)], axis=1
    ).reshape(ranks, 2 * group, record_duration)
    narrow = jnp.asarray(pair.reshape(2 * NF, record_duration)).astype(jnp.bfloat16)
    plane = (2, nx, ny, SUBS, LANES)
    square = pltpu.VMEM((depths * nx // group, LANES, LANES), jnp.float32)
    vmem = pl.BlockSpec(memory_space=pltpu.VMEM)
    hbm = pl.BlockSpec(memory_space=pl.ANY)
    near, rest = pl.pallas_call(
        functools.partial(migrate_kernel, group, class_count, ranks),
        out_shape=[jax.ShapeDtypeStruct((tile_rows, depths, width), jnp.float32)] * 2,
        in_specs=[hbm, vmem, hbm, vmem, vmem, vmem, vmem],
        out_specs=[vmem] * 2,
        scratch_shapes=[
            pltpu.VMEM((2,) + plane, jnp.float32),
            pltpu.VMEM((depths + 1,) + plane, jnp.float32),
            pltpu.VMEM((depths,) + plane[1:], jnp.int32),
            pltpu.VMEM((depths, degrees) + plane, jnp.float32),
            pltpu.VMEM((2, degrees, 2, SUBS, LANES), jnp.float32),
            pltpu.VMEM(plane, jnp.float32),
            square,
            square,
            pltpu.VMEM((ranks, tile_rows, SUBS, width), jnp.float32),
            pltpu.VMEM((depths, ranks * 16, width), jnp.float32),
            pltpu.VMEM((depths, ranks - 1, tile_rows, width), jnp.float32),
            pltpu.VMEM((tile_rows, record_duration, width), jnp.bfloat16),
            pltpu.VMEM((ranks, tile_rows, SUBS, width), jnp.float32),
            pltpu.VMEM((2 * group, record_duration), jnp.float32),
            pltpu.VMEM((2, SUBS, LANES), jnp.int32),
            pltpu.VMEM((SUBS, LANES), jnp.float32),
            pltpu.VMEM((group, degrees, SUBS, LANES), jnp.float32),
            pltpu.VMEM((degrees, SUBS, LANES), jnp.float32),
            pltpu.SemaphoreType.DMA,
            pltpu.SemaphoreType.DMA((tile_rows // 2,)),
            pltpu.SemaphoreType.DMA((2, ranks - 1)),
            pltpu.SemaphoreType.DMA((2, ranks - 1)),
            pltpu.SemaphoreType.DMA((depths, ranks - 1)),
            pltpu.SemaphoreType.DMA((depths, ranks - 1)),
        ],
        compiler_params=pltpu.CompilerParams(
            collective_id=0, has_side_effects=True, vmem_limit_bytes=VMEM_BYTES
        ),
        name="migrate",
    )(
        records[0].transpose(1, 0, 2),
        narrow,
        jnp.asarray(pair),
        wavelet,
        offsets[0].transpose(1, 2, 0),
        coefficients.transpose(1, 3, 2, 0),
        classes,
    )
    return (near + rest).transpose(1, 0, 2)


def dft_table(count, record_duration):
    spectral_slots = jnp.arange(count, dtype=jnp.int32) + first_bin
    clock_moments = jnp.arange(record_duration, dtype=jnp.int32)
    elementwise_multiple = spectral_slots[:, None] * clock_moments[None, :] % record_duration
    phase = elementwise_multiple.astype(jnp.float32) * (2.0 * math.pi / record_duration)
    scaling = 1.0 / math.sqrt(record_duration)
    stacked = jnp.stack([jnp.cos(phase), -jnp.sin(phase)], axis=1) * scaling
    return stacked.reshape(2 * count, record_duration)


def mcclellan(field):
    widths = [(0, 0)] * (field.ndim - 2) + [(1, 1), (1, 1)]
    zero_extended = jnp.pad(field, widths)
    along_x = (
        0.25 * zero_extended[..., :-2, :]
        + 0.5 * zero_extended[..., 1:-1, :]
        + 0.25 * zero_extended[..., 2:, :]
    )
    smoothed = 0.25 * along_x[..., :-2] + 0.5 * along_x[..., 1:-1] + 0.25 * along_x[..., 2:]
    return 2.0 * smoothed - field


def add_term(summed_terms, chebyshev, filters, degree):
    wavefield_polarity = jnp.array([1.0, -1.0], jnp.float32)[None, :, None, None, None]
    real_component = filters[:, 0, degree][:, None, None]
    im_part = filters[:, 1, degree][:, None, None] * wavefield_polarity
    cheb_re = chebyshev[:, :, :, 0]
    cheb_im = chebyshev[:, :, :, 1]
    return summed_terms + jnp.stack(
        [
            real_component * cheb_re - im_part * cheb_im,
            real_component * cheb_im + im_part * cheb_re,
        ],
        axis=3,
    )


def extrapolate(fields, filters):
    degrees = filters.shape[2]
    previous = fields
    current = mcclellan(fields)
    summed_terms = add_term(jnp.zeros_like(fields), previous, filters, 0)
    summed_terms = add_term(summed_terms, current, filters, 1)
    for degree in range(2, degrees):
        previous, current = (current, 2.0 * mcclellan(current) - previous)
        summed_terms = add_term(summed_terms, current, filters, degree)
    return summed_terms


def emitter_impulses(offsets, spacing, height, breadth):
    off_x = jnp.repeat(jnp.repeat(offsets[..., 0], spacing, axis=1), spacing, axis=2)
    off_y = jnp.repeat(jnp.repeat(offsets[..., 1], spacing, axis=1), spacing, axis=2)
    row_phase = jnp.arange(height, dtype=jnp.int32) % spacing
    col_phase = jnp.arange(breadth, dtype=jnp.int32) % spacing
    hits = (row_phase[None, :, None] == off_x) & (col_phase[None, None, :] == off_y)
    return hits.astype(jnp.float32)


def plain_device(records, wavelet, offsets, classes, coefficients):
    shot_count, record_duration, tile_rows, width_y = records.shape
    freq_local = coefficients.shape[1]
    fourier_matrix = dft_table(NF, record_duration)
    narrow_table = fourier_matrix.astype(jnp.bfloat16)
    spectra = jnp.stack(
        [
            jnp.dot(
                narrow_table,
                records[0].reshape(record_duration, tile_rows * width_y),
                preferred_element_type=jnp.float32,
            ).reshape(NF, 2, tile_rows, width_y)
        ],
        axis=1,
    )
    receivers = lax.all_to_all(spectra, "freq", split_axis=0, concat_axis=3, tiled=True)
    height = receivers.shape[3]
    wave_spec = (
        jnp.dot(wavelet, fourier_matrix.T, precision=lax.Precision.HIGHEST)
        .reshape(shot_count, NF, 2)
        .transpose(1, 0, 2)
    )
    first_freq = lax.axis_index("freq") * freq_local
    wave_local = lax.dynamic_slice_in_dim(wave_spec, first_freq, freq_local, 0)
    spikes = emitter_impulses(offsets, SPACING, height, width_y)
    source = wave_local[:, :, :, None, None] * spikes[None, :, None]
    fields = jnp.stack([source, receivers], axis=1)
    class_ids = jnp.arange(coefficients.shape[0], dtype=jnp.int32)
    migrated_pictures = []
    for level in range(classes.shape[0]):
        onehot = (classes[level][None] == class_ids[:, None, None]).astype(jnp.float32)
        filters = jnp.einsum(
            "cfrk,cxy->frkxy", coefficients, onehot, precision=lax.Precision.HIGHEST
        )
        fields = extrapolate(fields, filters)
        partial_value = jnp.sum(fields[:, 0] * fields[:, 1], axis=(0, 1, 2))
        migrated_pictures.append(
            lax.psum_scatter(partial_value, "freq", scatter_dimension=0, tiled=True)
        )
    return jnp.stack(migrated_pictures)


def fits_lanes(records, classes, coefficients):
    tile_rows, width = records.shape[2:]
    height = classes.shape[1]
    class_count, group = coefficients.shape[:2]
    return (
        2 * group == SUBS
        and width == LANES
        and width // SUBS == SPACING
        and group * class_count <= LANES
        and height * group % LANES == 0
        and height // tile_rows % 2 == 0
        and 2 * (height * group // LANES) == tile_rows
    )


def per_device(records, wavelet, offsets, classes, coefficients):
    if fits_lanes(records, classes, coefficients):
        return fast_device(records, wavelet, offsets, classes, coefficients)
    return plain_device(records, wavelet, offsets, classes, coefficients)


def solution(mesh):
    placed = (
        P("parts", None, "freq", None),
        P("parts", None),
        P("parts", None, None, None),
        P("parts", None, None),
        P(None, "freq", None, None),
    )
    return jax.shard_map(
        per_device, mesh=mesh, in_specs=placed, out_specs=P("parts", "freq", None), check_vma=False
    )
```

```python
import functools
import math

import jax
import jax.numpy as jnp
import numpy as np
from jax import lax
from jax.experimental import pallas as pl
from jax.experimental.pallas import tpu as pltpu
from jax.sharding import PartitionSpec as P

NF = 64
SPACING = 16
LANES = 128
SUBS = 8
VMEM_BYTES = 60 * 2**20
NODES = (0.75, 1.0)


first_bin = 4


def dft_rows(count, record_duration):
    slots = np.arange(count, dtype=np.int64) + first_bin
    moments = np.arange(record_duration, dtype=np.int64)
    phase = (slots[:, None] * moments[None, :] % record_duration).astype(np.float32)
    phase = phase * np.float32(2.0 * math.pi / record_duration)
    scaling = np.float32(1.0 / math.sqrt(record_duration))
    return np.cos(phase) * scaling, -np.sin(phase) * scaling


def basis_change(degrees):
    poly = np.polynomial.Polynomial
    basis = [poly([1.0])]
    for j in range(degrees - 1):
        node = NODES[j] if j < len(NODES) else 0.0
        basis.append(basis[-1] * poly([-16.0 * node, 16.0]))
    matrix = np.zeros((degrees, degrees))
    for j, b in enumerate(basis):
        matrix[: len(b.coef), j] = b.coef
    out = np.zeros((degrees, degrees))
    for k in range(degrees):
        shifted = np.polynomial.Chebyshev.basis(k).convert(kind=poly)(poly([-1.0, 2.0]))
        coef = np.zeros(degrees)
        coef[: len(shifted.coef)] = shifted.coef
        out[:, k] = np.linalg.solve(matrix, coef)
    return out


def iotas():
    lane = lax.broadcasted_iota(jnp.int32, (SUBS, LANES), 1)
    sub = lax.broadcasted_iota(jnp.int32, (SUBS, LANES), 0)
    return lane, sub


def pick(table, index):
    along_lanes = lax.GatherDimensionNumbers(
        offset_dims=(),
        collapsed_slice_dims=(1,),
        start_index_map=(1,),
        operand_batching_dims=(0,),
        start_indices_batching_dims=(0,),
    )
    return lax.gather(
        table,
        index[..., None],
        along_lanes,
        slice_sizes=(1, 1),
        mode=lax.GatherScatterMode.PROMISE_IN_BOUNDS,
    )


def row_of(tab, part, k):
    return jnp.broadcast_to(tab[k, pl.ds(part, 1), :], (SUBS, LANES))


def lane_classes(classes, idx, flat, group, class_count):
    depths, nx, ny = idx.shape[:3]
    blocks = LANES // group
    lane, _ = iotas()
    places = [(d, x) for d in range(depths) for x in range(nx)]
    for n in range(0, len(places), group):
        some = places[n : n + group]
        rows = [classes[d, pl.ds(x, blocks, stride=nx), :] for d, x in some]
        slot = n // group
        flat[slot] = jnp.transpose(jnp.concatenate(rows, axis=0).astype(jnp.float32))
        for i, (d, x) in enumerate(some):
            for y in range(ny):
                line = flat[slot, pl.ds(y, SUBS, stride=ny), :].astype(jnp.int32)
                idx[d, x, y] = pick(line, lane // group + i * blocks) + lane % group * class_count


def look_up(tab, idx, store, x, y):
    place = idx[x, y]
    for k in range(tab.shape[0]):
        for part in range(2):
            store(k, part, pick(row_of(tab, part, k), place))


def planes_at(filters, x, y):
    def store(k, part, value):
        filters[k, part, x, y] = value

    return store


def degree_pass(old, cur, planes, acc, filters, node, group, nx, ny, begin=None, beside=None, kept=None):
    lane, sub = iotas()
    low, high = lane >= group, lane < LANES - group
    first, last = sub >= 1, sub < SUBS - 1

    def along_x(c, y):
        v = [old[c, x, y] for x in range(nx)]
        before = jnp.where(low, pltpu.roll(v[nx - 1], group, 1), 0.0)
        after = jnp.where(high, pltpu.roll(v[0], LANES - group, 1), 0.0)
        ext = [before] + v + [after]
        pair = [ext[i] + ext[i + 1] for i in range(nx + 1)]
        return [pair[i] + pair[i + 1] for i in range(nx)]

    u, q, u_first = [], [], []
    for c in range(planes):
        end = along_x(c, ny - 1)
        prev = [jnp.where(first, pltpu.roll(e, 1, 0), 0.0) for e in end]
        start = along_x(c, 0)
        u.append(start)
        u_first.append(start)
        q.append([a + b for a, b in zip(prev, start)])
    for y in range(ny):
        made, was = [], []
        for c in range(planes):
            if y < ny - 1:
                nxt = along_x(c, y + 1)
            else:
                nxt = [jnp.where(last, pltpu.roll(e, SUBS - 1, 0), 0.0) for e in u_first[c]]
            q_next = [a + b for a, b in zip(u[c], nxt)]
            total = [a + b for a, b in zip(q[c], q_next)]
            if node is not None:
                held = [old[c, x, y] for x in range(nx)]
                total = [t - node * h for t, h in zip(total, held)]
                was.append(held)
                if kept is not None:
                    for x in range(nx):
                        kept[c, x, y] = held[x]
            for x in range(nx):
                cur[c, x, y] = total[x]
            made.append(total)
            u[c], q[c] = nxt, q_next
        for x in range(nx):
            hr, hi = filters[0, x, y], filters[1, x, y]
            if planes == 2:
                re, im = made[0][x], made[1][x]
                if begin is None:
                    acc[0, x, y] = acc[0, x, y] + (hr * re - hi * im)
                    acc[1, x, y] = acc[1, x, y] + (hr * im + hi * re)
                else:
                    gr, gi = begin[0, x, y], begin[1, x, y]
                    was_re, was_im = was[0][x], was[1][x]
                    acc[0, x, y] = (gr * was_re - gi * was_im) + (hr * re - hi * im)
                    acc[1, x, y] = (gr * was_im + gi * was_re) + (hr * im + hi * re)
            else:
                acc[0, x, y] = acc[0, x, y] + hr * made[0][x]
                acc[1, x, y] = acc[1, x, y] + hi * made[0][x]
        if beside is not None:
            beside(y)


def node_at(j):
    node = jnp.float32(16.0 * NODES[-1])
    for n, value in enumerate(NODES[:-1]):
        node = jnp.where(j == n, jnp.float32(16.0 * value), node)
    return node


def spread_ahead(ahead, steps, j, nx, ny):
    if ahead is None:
        return None
    tab, idx, filters, staged = ahead
    share, slots = nx * ny // steps, 0 if staged is None else staged.shape[0]

    def at(n):
        return n % nx, j * (share // nx) + n // nx

    def flush(n):
        for k in range(tab.shape[0]):
            for part in range(2):
                filters[(k, part) + at(n)] = staged[n % slots, k, part]

    def beside(y):
        for n in range(share * y // ny, share * (y + 1) // ny):
            if staged is None:
                look_up(tab, idx, planes_at(filters, *at(n)), *at(n))
                continue
            if n >= slots:
                flush(n - slots)

            def store(k, part, value):
                staged[n % slots, k, part] = value

            look_up(tab, idx, store, *at(n))
        if y == ny - 1 and staged is not None:
            for n in range(share - slots, share):
                flush(n)

    return beside


def all_degrees(cur, planes, acc, filters, group, nx, ny, ahead=None, fresh=False, kept=None):
    steps = filters.shape[0] - 1
    def one(shifted, j, carry):
        degree_pass(
            cur, cur, planes, acc, filters.at[j + 1], node_at(j) if shifted else None,
            group, nx, ny, None, spread_ahead(ahead, steps, j, nx, ny),
        )
        return carry

    done = 0
    if fresh:
        degree_pass(
            acc, cur, planes, acc, filters.at[1], 16.0 * NODES[0], group, nx, ny,
            filters.at[0], spread_ahead(ahead, steps, 0, nx, ny), kept,
        )
        one(True, 1, 0)
    else:
        lax.fori_loop(0, len(NODES), functools.partial(one, True), 0)
    lax.fori_loop(len(NODES), steps, functools.partial(one, False), 0)


def source_steps(group, off_ref, wave, tab, out, kept, idx, filters, cur, staged):
    depths, nx, ny = idx.shape[:3]
    lane, _ = iotas()

    row_x = [lane // group * nx + x for x in range(nx)]
    off_x = [pick(off_ref[0], r // SPACING) for r in row_x]
    off_y = [pick(off_ref[1], r // SPACING) for r in row_x]

    def spike_row(y, carry):
        for x in range(nx):
            hit = (row_x[x] % SPACING == off_x[x]) & (off_y[x] == y)
            v = jnp.where(hit, 1.0, 0.0)
            cur[0, x, y] = v
            out[0, x, y] = filters[0, 0, 0, x, y] * v
            out[1, x, y] = filters[0, 0, 1, x, y] * v
        return carry

    lax.fori_loop(0, ny, spike_row, 0, unroll=4)

    def ahead_of(d, staged=None):
        return tab, idx.at[d], filters.at[d], staged

    all_degrees(cur, 1, out, filters.at[0], group, nx, ny, ahead_of(1, staged))
    wr, wi = jnp.zeros((SUBS, LANES), jnp.float32), jnp.zeros((SUBS, LANES), jnp.float32)
    for f in range(group):
        wr = jnp.where(lane % group == f, jnp.broadcast_to(wave[pl.ds(f, 1), :], wr.shape), wr)
        wi = jnp.where(
            lane % group == f, -jnp.broadcast_to(wave[pl.ds(group + f, 1), :], wi.shape), wi
        )

    def wave_row(y, carry):
        for x in range(nx):
            re, im = out[0, x, y], out[1, x, y]
            out[0, x, y] = wr * re - wi * im
            out[1, x, y] = wr * im + wi * re
        return carry

    lax.fori_loop(0, ny, wave_row, 0, unroll=4)

    def depth(d, carry):
        filter_step(group, cur, out, filters.at[d], kept.at[d - 1], ahead_of(d + 1))
        return carry

    lax.fori_loop(1, depths - 1, depth, 0)


def filter_step(group, cur, field, filters, kept, ahead=None):
    nx, ny = field.shape[1:3]
    all_degrees(cur, 2, field, filters, group, nx, ny, ahead, True, kept)


def small_tables(offsets, wavelet, coefs, off, wave, tab, wide, moments):
    group, degrees, _, class_count = coefs.shape
    rows, columns = offsets.shape[0], offsets.shape[2]
    for by in range(rows):
        for c in range(2):
            off[c, pl.ds(by, 1), pl.ds(0, columns)] = offsets[by, pl.ds(c, 1), :]
    wave[...] = jnp.broadcast_to(
        jnp.sum(moments[...] * wavelet[...], axis=1, keepdims=True), wave.shape
    )
    wide[...] = jnp.zeros_like(wide)
    for f in range(group):
        for k in range(degrees):
            wide[f, k, pl.ds(0, 2), pl.ds(0, class_count)] = coefs[f, k]
    joined = []
    for k in range(degrees):
        row = wide[0, k]
        for f in range(1, group):
            row = row + pltpu.roll(wide[f, k], f * class_count, 1)
        joined.append(row)
    change = basis_change(degrees)
    for j in range(degrees):
        total = None
        for k in range(degrees):
            if change[j, k] != 0.0:
                term = np.float32(change[j, k]) * joined[k]
                total = term if total is None else total + term
        tab[j] = total


def exchange_peers(ranks):
    me = lax.axis_index("freq")
    return me, [lax.rem(me + k, ranks) for k in range(1, ranks)]


def remote(src, dst, send, recv, peer):
    return pltpu.make_async_remote_copy(
        src_ref=src,
        dst_ref=dst,
        send_sem=send,
        recv_sem=recv,
        device_id={"freq": peer},
        device_id_type=pl.DeviceIdType.MESH,
    )


def unpack_received(received, acc, flat, group, nx, ny):
    senders = received.shape[0]
    sub3 = lax.broadcasted_iota(jnp.int32, (senders, SUBS, LANES), 1)
    upper = sub3 < group
    for x in range(nx):
        a, b = received[:, x], received[:, nx + x]
        parts = (
            jnp.where(upper, a, pltpu.roll(b, group, 1)),
            jnp.where(upper, pltpu.roll(a, group, 1), b),
        )
        for r in range(2):
            flat[r] = jnp.transpose(parts[r].reshape(LANES, LANES))
            for y in range(ny):
                acc[r, x, y] = flat[r, pl.ds(y, SUBS, stride=ny), :]


def form_image(src, acc, flat, turned, image, group, nx, ny):
    owners = image.shape[0] // 16
    for x in range(nx):
        for y in range(ny):
            v = src[0, x, y] * acc[0, x, y] - src[1, x, y] * acc[1, x, y]
            flat[x, pl.ds(y, SUBS, stride=ny), :] = v
        turned[x] = jnp.transpose(flat[x])
        for b in range(2):
            total = turned[x, pl.ds(b * group, owners, stride=2 * group), :]
            for f in range(1, group):
                total = total + turned[x, pl.ds(b * group + f, owners, stride=2 * group), :]
            image[pl.ds(b * nx + x, owners, stride=16), :] = total


def migrate_kernel(
    group, class_count, ranks,
    records, table, moments_all, wavelet, offsets, coefs, classes,
    near, rest,
    fields, kept, idx, filters, staged, cur, flat, turned, received, image, slots,
    traces, spectra, moments, off, wave, wide, tab,
    local_sem, rec_sem, a_send, a_recv, i_send, i_recv,
):
    depths, nx, ny = idx.shape[:3]
    tile = records.shape[0]
    halves, pairs = 2, tile // 4
    me, peers = exchange_peers(ranks)
    barrier = pltpu.get_barrier_semaphore()
    for peer in peers:
        pl.semaphore_signal(
            barrier, inc=1, device_id={"freq": peer}, device_id_type=pl.DeviceIdType.MESH
        )
    mine = pltpu.make_async_copy(moments_all.at[me], moments, local_sem)
    mine.start()

    def load(p):
        rows = pl.ds(2 * p, 2)
        return pltpu.make_async_copy(records.at[rows], traces.at[rows], rec_sem.at[p])

    for p in range(halves * pairs):
        load(p).start()
    mine.wait()
    small_tables(offsets, wavelet, coefs, off, wave, tab, wide, moments)
    lane_classes(classes, idx, flat, group, class_count)
    pl.semaphore_wait(barrier, ranks - 1)

    def spread(half):
        rows = pl.ds(half * 2 * pairs, 2 * pairs)
        return [
            remote(
                spectra.at[peer, rows],
                received.at[me, rows],
                a_send.at[half, k],
                a_recv.at[half, k],
                peer,
            )
            for k, peer in enumerate(peers)
        ]

    def transform(half, carry):
        def pair(i, carry):
            p = half * pairs + i
            load(p).wait()
            both = jnp.concatenate([traces[2 * p], traces[2 * p + 1]], axis=1)
            made = jnp.dot(table[...], both, preferred_element_type=jnp.float32)
            width = made.shape[1] // 2
            for n in range(2):
                spectra[:, 2 * p + n] = made[:, n * width : (n + 1) * width].reshape(
                    ranks, SUBS, width
                )
            share = nx * ny // (halves * pairs)
            for n in range(share):
                at = p * share + n
                look_up(tab, idx.at[0], planes_at(filters.at[0], at // ny, at % ny), at // ny, at % ny)
            return carry

        lax.fori_loop(0, pairs, pair, 0)
        for copy in spread(half):
            copy.start()
        return carry

    lax.fori_loop(0, halves, transform, 0)
    own = pltpu.make_async_copy(spectra.at[me], received.at[me], local_sem)
    own.start()
    source_steps(group, off, wave, tab, fields.at[0], kept, idx, filters, cur, staged)
    acc = fields.at[1]

    def sends(d):
        return [
            remote(
                image.at[d, pl.ds(peer * 16, tile)],
                slots.at[d, k],
                i_send.at[d, k],
                i_recv.at[d, k],
                peer,
            )
            for k, peer in enumerate(peers)
        ]

    def step(n, carry):
        @pl.when(n == 1)
        def _():
            own.wait()
            for half in range(halves):
                for copy in spread(half):
                    copy.wait()
            kept[depths - 1] = fields[0]
            unpack_received(received, acc, flat, group, nx, ny)

        ready = jnp.minimum(n, 1)
        d = (depths - 1) * (1 - ready) + (n - 1) * ready
        spare = (depths - 2) * (1 - ready) + depths * ready
        filter_step(group, cur, fields.at[ready], filters.at[d], kept.at[spare])

        @pl.when(n >= 1)
        def _():
            form_image(kept.at[d], acc, flat, turned, image.at[d], group, nx, ny)
            for copy in sends(d):
                copy.start()

        return carry

    lax.fori_loop(0, depths + 1, step, 0)
    for d in range(depths):
        copies = sends(d)
        for copy in copies:
            copy.wait_send()
        sums = [image[d, pl.ds(me * 16, tile), :], None]
        for k, copy in enumerate(copies):
            copy.wait_recv()
            n = k * 2 // ranks
            sums[n] = slots[d, k] if sums[n] is None else sums[n] + slots[d, k]
        near[:, d, :] = sums[0]
        rest[:, d, :] = sums[1]


def fast_device(records, wavelet, offsets, classes, coefficients):
    _, record_duration, tile_rows, width = records.shape
    depths, height, _ = classes.shape
    class_count, group, _, degrees = coefficients.shape
    ranks = height // tile_rows
    nx, ny = group * height // LANES, width // SUBS
    cos_rows, sin_rows = dft_rows(NF, record_duration)
    pair = np.stack(
        [cos_rows.reshape(ranks, group, -1), -sin_rows.reshape(ranks, group, -1)], axis=1
    ).reshape(ranks, 2 * group, record_duration)
    narrow = jnp.asarray(pair.reshape(2 * NF, record_duration)).astype(jnp.bfloat16)
    plane = (2, nx, ny, SUBS, LANES)
    square = pltpu.VMEM((depths * nx // group, LANES, LANES), jnp.float32)
    vmem = pl.BlockSpec(memory_space=pltpu.VMEM)
    hbm = pl.BlockSpec(memory_space=pl.ANY)
    near, rest = pl.pallas_call(
        functools.partial(migrate_kernel, group, class_count, ranks),
        out_shape=[jax.ShapeDtypeStruct((tile_rows, depths, width), jnp.float32)] * 2,
        in_specs=[hbm, vmem, hbm, vmem, vmem, vmem, vmem],
        out_specs=[vmem] * 2,
        scratch_shapes=[
            pltpu.VMEM((2,) + plane, jnp.float32),
            pltpu.VMEM((depths + 1,) + plane, jnp.float32),
            pltpu.VMEM((depths,) + plane[1:], jnp.int32),
            pltpu.VMEM((depths, degrees) + plane, jnp.float32),
            pltpu.VMEM((2, degrees, 2, SUBS, LANES), jnp.float32),
            pltpu.VMEM(plane, jnp.float32),
            square,
            square,
            pltpu.VMEM((ranks, tile_rows, SUBS, width), jnp.float32),
            pltpu.VMEM((depths, ranks * 16, width), jnp.float32),
            pltpu.VMEM((depths, ranks - 1, tile_rows, width), jnp.float32),
            pltpu.VMEM((tile_rows, record_duration, width), jnp.bfloat16),
            pltpu.VMEM((ranks, tile_rows, SUBS, width), jnp.float32),
            pltpu.VMEM((2 * group, record_duration), jnp.float32),
            pltpu.VMEM((2, SUBS, LANES), jnp.int32),
            pltpu.VMEM((SUBS, LANES), jnp.float32),
            pltpu.VMEM((group, degrees, SUBS, LANES), jnp.float32),
            pltpu.VMEM((degrees, SUBS, LANES), jnp.float32),
            pltpu.SemaphoreType.DMA,
            pltpu.SemaphoreType.DMA((tile_rows // 2,)),
            pltpu.SemaphoreType.DMA((2, ranks - 1)),
            pltpu.SemaphoreType.DMA((2, ranks - 1)),
            pltpu.SemaphoreType.DMA((depths, ranks - 1)),
            pltpu.SemaphoreType.DMA((depths, ranks - 1)),
        ],
        compiler_params=pltpu.CompilerParams(
            collective_id=0, has_side_effects=True, vmem_limit_bytes=VMEM_BYTES
        ),
        name="migrate",
    )(
        records[0].transpose(1, 0, 2),
        narrow,
        jnp.asarray(pair),
        wavelet,
        offsets[0].transpose(1, 2, 0),
        coefficients.transpose(1, 3, 2, 0),
        classes,
    )
    return (near + rest).transpose(1, 0, 2)


def dft_table(count, record_duration):
    spectral_slots = jnp.arange(count, dtype=jnp.int32) + first_bin
    clock_moments = jnp.arange(record_duration, dtype=jnp.int32)
    elementwise_multiple = spectral_slots[:, None] * clock_moments[None, :] % record_duration
    phase = elementwise_multiple.astype(jnp.float32) * (2.0 * math.pi / record_duration)
    scaling = 1.0 / math.sqrt(record_duration)
    stacked = jnp.stack([jnp.cos(phase), -jnp.sin(phase)], axis=1) * scaling
    return stacked.reshape(2 * count, record_duration)


def mcclellan(field):
    widths = [(0, 0)] * (field.ndim - 2) + [(1, 1), (1, 1)]
    zero_extended = jnp.pad(field, widths)
    along_x = (
        0.25 * zero_extended[..., :-2, :]
        + 0.5 * zero_extended[..., 1:-1, :]
        + 0.25 * zero_extended[..., 2:, :]
    )
    smoothed = 0.25 * along_x[..., :-2] + 0.5 * along_x[..., 1:-1] + 0.25 * along_x[..., 2:]
    return 2.0 * smoothed - field


def add_term(summed_terms, chebyshev, filters, degree):
    wavefield_polarity = jnp.array([1.0, -1.0], jnp.float32)[None, :, None, None, None]
    real_component = filters[:, 0, degree][:, None, None]
    im_part = filters[:, 1, degree][:, None, None] * wavefield_polarity
    cheb_re = chebyshev[:, :, :, 0]
    cheb_im = chebyshev[:, :, :, 1]
    return summed_terms + jnp.stack(
        [
            real_component * cheb_re - im_part * cheb_im,
            real_component * cheb_im + im_part * cheb_re,
        ],
        axis=3,
    )


def extrapolate(fields, filters):
    degrees = filters.shape[2]
    previous = fields
    current = mcclellan(fields)
    summed_terms = add_term(jnp.zeros_like(fields), previous, filters, 0)
    summed_terms = add_term(summed_terms, current, filters, 1)
    for degree in range(2, degrees):
        previous, current = (current, 2.0 * mcclellan(current) - previous)
        summed_terms = add_term(summed_terms, current, filters, degree)
    return summed_terms


def emitter_impulses(offsets, spacing, height, breadth):
    off_x = jnp.repeat(jnp.repeat(offsets[..., 0], spacing, axis=1), spacing, axis=2)
    off_y = jnp.repeat(jnp.repeat(offsets[..., 1], spacing, axis=1), spacing, axis=2)
    row_phase = jnp.arange(height, dtype=jnp.int32) % spacing
    col_phase = jnp.arange(breadth, dtype=jnp.int32) % spacing
    hits = (row_phase[None, :, None] == off_x) & (col_phase[None, None, :] == off_y)
    return hits.astype(jnp.float32)


def plain_device(records, wavelet, offsets, classes, coefficients):
    shot_count, record_duration, tile_rows, width_y = records.shape
    freq_local = coefficients.shape[1]
    fourier_matrix = dft_table(NF, record_duration)
    narrow_table = fourier_matrix.astype(jnp.bfloat16)
    spectra = jnp.stack(
        [
            jnp.dot(
                narrow_table,
                records[0].reshape(record_duration, tile_rows * width_y),
                preferred_element_type=jnp.float32,
            ).reshape(NF, 2, tile_rows, width_y)
        ],
        axis=1,
    )
    receivers = lax.all_to_all(spectra, "freq", split_axis=0, concat_axis=3, tiled=True)
    height = receivers.shape[3]
    wave_spec = (
        jnp.dot(wavelet, fourier_matrix.T, precision=lax.Precision.HIGHEST)
        .reshape(shot_count, NF, 2)
        .transpose(1, 0, 2)
    )
    first_freq = lax.axis_index("freq") * freq_local
    wave_local = lax.dynamic_slice_in_dim(wave_spec, first_freq, freq_local, 0)
    spikes = emitter_impulses(offsets, SPACING, height, width_y)
    source = wave_local[:, :, :, None, None] * spikes[None, :, None]
    fields = jnp.stack([source, receivers], axis=1)
    class_ids = jnp.arange(coefficients.shape[0], dtype=jnp.int32)
    migrated_pictures = []
    for level in range(classes.shape[0]):
        onehot = (classes[level][None] == class_ids[:, None, None]).astype(jnp.float32)
        filters = jnp.einsum(
            "cfrk,cxy->frkxy", coefficients, onehot, precision=lax.Precision.HIGHEST
        )
        fields = extrapolate(fields, filters)
        partial_value = jnp.sum(fields[:, 0] * fields[:, 1], axis=(0, 1, 2))
        migrated_pictures.append(
            lax.psum_scatter(partial_value, "freq", scatter_dimension=0, tiled=True)
        )
    return jnp.stack(migrated_pictures)


def fits_lanes(records, classes, coefficients):
    tile_rows, width = records.shape[2:]
    height = classes.shape[1]
    class_count, group = coefficients.shape[:2]
    return (
        2 * group == SUBS
        and width == LANES
        and width // SUBS == SPACING
        and group * class_count <= LANES
        and height * group % LANES == 0
        and height // tile_rows % 2 == 0
        and 2 * (height * group // LANES) == tile_rows
    )


def per_device(records, wavelet, offsets, classes, coefficients):
    if fits_lanes(records, classes, coefficients):
        return fast_device(records, wavelet, offsets, classes, coefficients)
    return plain_device(records, wavelet, offsets, classes, coefficients)


def solution(mesh):
    placed = (
        P("parts", None, "freq", None),
        P("parts", None),
        P("parts", None, None, None),
        P("parts", None, None),
        P(None, "freq", None, None),
    )
    return jax.shard_map(
        per_device, mesh=mesh, in_specs=placed, out_specs=P("parts", "freq", None), check_vma=False
    )
```
